32 devices in a mesh: wide: 16 (over z, y, x), narrow: 2 (over core).
Axes of the slice: x: 2, y: 2, z: 4, core: 2. Of those that a mesh axis runs over, the one named last changes fastest.
Arguments:
- residual_local: float32 [256, 32, 128], P('wide', 'narrow'), may hold values from -6 to 6
- geometry: float32 [3, 256, 32, 128], P(None, 'wide', 'narrow'), may hold values from 0.02 to 0.2
- helmholtz: float32 [256, 32, 128], P('wide', 'narrow'), may hold values from 0.2 to 2
- coarse_ids: int32 [32, 4, 16, 8], P('wide', 'narrow'), may hold values from 1 to 255, as said below
- coarse_correction: float32 [4096], P(('wide', 'narrow')), may hold values from -6 to 6
Outputs:
- preconditioned: float32 [256, 32, 128], P('wide', 'narrow')
- coarse_residual: float32 [4096], P(('wide', 'narrow'))
The draws below stay inside these ranges and needn't reach their ends.
Inputs may be any that keep to these rules, and one draw needn't show every extreme that they name: `coarse_ids`: within one slab (2 consecutive element planes along the first dimension) the ids number the slab's corner points one to one: corners that elements of the slab share carry the same id, distinct corner points distinct ids. Each slab has its own numbering.
All inputs are finite; a program needn't handle non-finite values.
Results may differ from the reference program's by a relative error of at most 0.0003.
Values sent between devices are 32-bit elements; how exact they have to be, the bound alone decides.
A program may use at most 64 MiB of HBM per device.

```python
import math
import jax
import jax.numpy as jnp
import numpy as np
from jax import lax

NODES = 8
DEGREE = 3
EXD = 2
ELEMENTS_FIRST = 32
ELEMENTS_SECOND = 4
ELEMENTS_THIRD = 16
NX = 256
NY = 32
NZ = 128
NVERT = 255
COARSE = 256
COARSE_ALL = 4096
N_WIDE = 16


def draw_coarse_ids(key, part):
    slabs = ELEMENTS_FIRST // EXD
    corner = jnp.arange(8, dtype=jnp.int32)
    first_direction = corner // 4
    second_direction = corner // 2 % 2
    third_direction = corner % 2
    element_first = jnp.arange(EXD, dtype=jnp.int32)[:, None, None, None]
    element_second = jnp.arange(ELEMENTS_SECOND, dtype=jnp.int32)[None, :, None, None]
    element_third = jnp.arange(ELEMENTS_THIRD, dtype=jnp.int32)[None, None, :, None]
    element_mesh = ((element_first + first_direction) * (ELEMENTS_SECOND + 1) + element_second + second_direction) * (ELEMENTS_THIRD + 1) + element_third + third_direction

    def one_slab(index):
        order = jax.random.permutation(jax.random.fold_in(key, index), NVERT).astype(jnp.int32)
        return COARSE - 1 - order[element_mesh]
    element_blocks = jax.vmap(one_slab)(jnp.arange(slabs, dtype=jnp.int32))
    return element_blocks.reshape(ELEMENTS_FIRST, ELEMENTS_SECOND, ELEMENTS_THIRD, 8).astype(jnp.int32)


def shard_levels(key, shape, split, low, top_value):
    loudness, own = 1.0, jax.random.fold_in(key, 6)
    for position, blocks in split:
        steps = jnp.exp(jax.random.uniform(jax.random.fold_in(own, position), (blocks,), jnp.float32, low / len(split), top_value / len(split)))
        loudness = loudness * jnp.repeat(steps, shape[position] // blocks).reshape([-1 if axis == position else 1 for axis in range(len(shape))])
    return loudness


def gaussian(key, shape, scale, bound, shards=(), kind=jnp.bfloat16):
    entries = scale * jax.random.normal(key, shape, jnp.float32)
    if shards:
        entries = entries * shard_levels(key, shape, shards, -0.22, 0.18)
    return jnp.clip(entries, -bound, bound).astype(kind)


def setup_inputs(seed: int = 0) -> dict:
    keys = jax.random.split(jax.random.key(seed), 6)
    residual_local = gaussian(keys[0], (NX, NY, NZ), 1.0, 6.0, ((0, 16), (1, 2)), jnp.float32)
    geometry = jnp.clip(jnp.exp(math.log(0.2) - 2.3025851 * jax.random.uniform(keys[1], (3, NX, NY, NZ), jnp.float32) ** shard_levels(keys[1], (3, NX, NY, NZ), ((1, 16), (2, 2)), -0.2, 0.2)), 0.02, 0.2)
    helmholtz = jnp.clip(jnp.exp(math.log(2.0) - 2.3025851 * jax.random.uniform(keys[2], (NX, NY, NZ), jnp.float32) ** shard_levels(keys[2], (NX, NY, NZ), ((0, 16), (1, 2)), -0.2, 0.2)), 0.2, 2.0)
    coarse_ids = draw_coarse_ids(jax.random.fold_in(keys[5], 71), 0)
    coarse_correction = gaussian(keys[4], (COARSE_ALL,), 1.0, 6.0, ((0, 32),), jnp.float32)
    return {"residual_local": residual_local, "geometry": geometry, "helmholtz": helmholtz, "coarse_ids": coarse_ids, "coarse_correction": coarse_correction}


low_bound = 0.3
high_bound = 3.3
gll_inner = (-0.8717401485096066, -0.5917001814331423, -0.2092992179024789, 0.2092992179024789, 0.5917001814331423, 0.8717401485096066)


def legendre_values(points, order):
    previous = points * 0.0 + 1.0
    current = points
    for number in range(1, order):
        previous, current = current, ((2 * number + 1) * points * current - number * previous) / (number + 1)
    return current


def tables():
    order = NODES - 1
    points = np.concatenate([np.array([-1.0]), np.array(gll_inner), np.array([1.0])])
    values = legendre_values(points, order)
    eye = np.eye(NODES)
    differ = points[:, None] - points[None, :] + eye
    offdiag = np.where(eye > 0, 0.0, values[:, None] / values[None, :] / differ)
    ends = np.concatenate([np.array([-order * (order + 1) / 4.0]), np.zeros(NODES - 2), np.array([order * (order + 1) / 4.0])])
    derivative = offdiag + eye * ends[None, :]
    linear = np.stack([(1.0 - points) / 2.0, (1.0 + points) / 2.0], axis=1)
    return jnp.asarray(derivative, dtype=jnp.float32), jnp.asarray(linear, dtype=jnp.float32)


def element_operator(field, geometry, helmholtz, derivative, block):
    highest = lax.Precision.HIGHEST
    sx, sy, sz = field.shape
    first = field.reshape(sx // NODES, NODES, sy, sz)
    grads = jnp.einsum('ab,ebyz->eayz', derivative, first, precision=highest) * geometry[0].reshape(first.shape)
    result = jnp.einsum('ab,eayz->ebyz', derivative, grads, precision=highest).reshape(field.shape)
    second = field.reshape(sx, sy // NODES, NODES, sz)
    grads = jnp.einsum('ab,xebz->xeaz', derivative, second, precision=highest) * geometry[1].reshape(second.shape)
    result = result + jnp.einsum('ab,xeaz->xebz', derivative, grads, precision=highest).reshape(field.shape)
    forward = jnp.kron(jnp.eye(block // NODES, dtype=jnp.float32), derivative)
    third = field.reshape(sx, sy, sz // block, block)
    grads = jnp.einsum('xyek,nk->xyen', third, forward, precision=highest) * geometry[2].reshape(third.shape)
    result = result + jnp.einsum('xyen,nk->xyek', grads, forward, precision=highest).reshape(field.shape)
    return result + helmholtz * field


def diagonal_part(geometry, helmholtz, derivative, block):
    highest = lax.Precision.HIGHEST
    sx, sy, sz = helmholtz.shape
    square = derivative * derivative
    result = jnp.einsum('ai,eayz->eiyz', square, geometry[0].reshape(sx // NODES, NODES, sy, sz), precision=highest).reshape(helmholtz.shape)
    result = result + jnp.einsum('ai,xeaz->xeiz', square, geometry[1].reshape(sx, sy // NODES, NODES, sz), precision=highest).reshape(helmholtz.shape)
    squares = jnp.kron(jnp.eye(block // NODES, dtype=jnp.float32), square)
    result = result + jnp.einsum('xyen,ni->xyei', geometry[2].reshape(sx, sy, sz // block, block), squares, precision=highest).reshape(helmholtz.shape)
    return result + helmholtz


def face_add(padded, axis, length):
    lower = lax.slice_in_dim(padded, 0, length, axis=axis)
    centre = lax.slice_in_dim(padded, 1, length + 1, axis=axis)
    upper = lax.slice_in_dim(padded, 2, length + 2, axis=axis)
    dims = [1] * padded.ndim
    dims[axis] = length
    places = (jnp.arange(length, dtype=jnp.int32) % NODES).reshape(dims)
    return centre + jnp.where(places == 0, lower, 0.0) + jnp.where(places == NODES - 1, upper, 0.0)


def assemble(field):
    for axis in range(3):
        widths = [(0, 0), (0, 0), (0, 0)]
        widths[axis] = (1, 1)
        field = face_add(jnp.pad(field, widths), axis, field.shape[axis])
    return field


def inverse_counts(dims_all, starts, totals):
    factors = []
    for axis in range(3):
        length = dims_all[axis]
        places = jnp.arange(length, dtype=jnp.int32)
        spots = starts[axis] + places
        inner = ((places % NODES == 0) & (spots > 0)) | ((places % NODES == NODES - 1) & (spots < totals[axis] - 1))
        dims = [1, 1, 1]
        dims[axis] = length
        factors.append(jnp.where(inner, 2.0, 1.0).astype(jnp.float32).reshape(dims))
    return 1.0 / (factors[0] * factors[1] * factors[2])


def restrict(field, linear, block):
    highest = lax.Precision.HIGHEST
    sx, sy, sz = field.shape
    expand = jnp.kron(jnp.eye(block // NODES, dtype=jnp.float32), linear)
    along_z = jnp.einsum('xyek,kc->xyec', field.reshape(sx, sy, sz // block, block), expand, precision=highest).reshape(sx, sy, sz // 4)
    along_y = jnp.einsum('jb,xejz->xebz', linear, along_z.reshape(sx, sy // NODES, NODES, sz // 4), precision=highest)
    along_x = jnp.einsum('ia,eiybz->eaybz', linear, along_y.reshape(sx // NODES, NODES, sy // NODES, 2, sz // 4), precision=highest)
    cube = along_x.reshape(sx // NODES, 2, sy // NODES, 2, sz // NODES, 2).transpose(0, 2, 4, 1, 3, 5)
    return cube.reshape(sx // NODES, sy // NODES, sz // NODES, 8)


def prolong(corners, linear, block, sx, sy, sz):
    highest = lax.Precision.HIGHEST
    cube = corners.reshape(sx // NODES, sy // NODES, sz // NODES, 2, 2, 2).transpose(0, 3, 1, 4, 2, 5)
    cube = cube.reshape(sx // NODES, 2, sy // NODES, 2, sz // 4)
    along_x = jnp.einsum('ia,eaybz->eiybz', linear, cube, precision=highest).reshape(sx, sy // NODES, 2, sz // 4)
    along_y = jnp.einsum('jb,xebz->xejz', linear, along_x, precision=highest).reshape(sx, sy, sz // block, block // 4)
    expand = jnp.kron(jnp.eye(block // NODES, dtype=jnp.float32), linear)
    return jnp.einsum('xyec,kc->xyek', along_y, expand, precision=highest).reshape(sx, sy, sz)


def chebyshev(residual, inv_diagonal, apply_operator, count, applies):
    theta = 0.5 * (high_bound + low_bound)
    delta = 0.5 * (high_bound - low_bound)
    sigma = theta / delta
    rho = 1.0 / sigma
    update = inv_diagonal * residual / theta
    solution = jnp.zeros_like(residual)
    for number in range(count):
        solution = solution + update
        if number < applies:
            residual = residual - apply_operator(update)
            if number + 1 < count:
                rho_next = 1.0 / (2.0 * sigma - rho)
                update = rho_next * rho * update + (2.0 * rho_next / delta) * inv_diagonal * residual
                rho = rho_next
    return solution, residual


def reference(residual_local, geometry, helmholtz, coarse_ids, coarse_correction):
    derivative, linear = tables()
    sx, sy, sz = residual_local.shape
    block = math.gcd(sz, 128)
    width = EXD * NODES

    def by_slab(local_fn):
        def one(index):
            start = (index * width).astype(jnp.int32)
            return local_fn(lax.dynamic_slice_in_dim(geometry, start, width, 1), lax.dynamic_slice_in_dim(helmholtz, start, width, 0), start)
        return lax.map(one, jnp.arange(N_WIDE, dtype=jnp.int32)).reshape(residual_local.shape)

    def apply_operator(field):
        def local_fn(geo_piece, helm_piece, start):
            piece = lax.dynamic_slice_in_dim(field, start, width, 0)
            return element_operator(piece, geo_piece, helm_piece, derivative, block)
        return assemble(by_slab(local_fn))

    def diag_fn(geo_piece, helm_piece, start):
        return diagonal_part(geo_piece, helm_piece, derivative, block)

    inv_diagonal = 1.0 / assemble(by_slab(diag_fn))
    rhs = assemble(residual_local)
    smoothed, pre_residual = chebyshev(rhs, inv_diagonal, apply_operator, DEGREE, DEGREE)
    weights = inverse_counts((sx, sy, sz), (0, 0, 0), (sx, sy, sz))
    corners = restrict(pre_residual * weights, linear, block)
    offsets = ((jnp.arange(ELEMENTS_FIRST, dtype=jnp.int32) // EXD) * COARSE).astype(jnp.int32)[:, None, None, None]
    slots = (coarse_ids + offsets).astype(jnp.int32)
    coarse_residual = jax.ops.segment_sum(corners.reshape(-1), slots.reshape(-1), num_segments=COARSE_ALL)
    correction = prolong(coarse_correction[slots], linear, block, sx, sy, sz)
    combined = smoothed + correction
    post_residual = pre_residual - apply_operator(correction)
    smoothing, unused = chebyshev(post_residual, inv_diagonal, apply_operator, DEGREE, DEGREE - 1)
    return combined + smoothing, coarse_residual
```

```python
import functools
import math

import jax
import jax.numpy as jnp
import numpy as np
from jax import lax
from jax.experimental import pallas as pl
from jax.experimental.pallas import tpu as pltpu
from jax.sharding import PartitionSpec as P

NODES = 8
DEGREE = 3
MESH = pl.DeviceIdType.MESH
HIGHEST = lax.Precision.HIGHEST

low_bound = 0.3
high_bound = 3.3
gll_inner = (
    -0.8717401485096066,
    -0.5917001814331423,
    -0.2092992179024789,
    0.2092992179024789,
    0.5917001814331423,
    0.8717401485096066,
)

DIRS = ((-1, 0), (1, 0), (-1, -1), (-1, 1), (1, -1), (1, 1), (0, -1), (0, 1))
OPPOSITE = tuple(DIRS.index((-a, -b)) for a, b in DIRS)

DIAG, RES, CORR, FIRST = 0, 1, 2, 3
FIELDS = FIRST + 2 * DEGREE - 1


def legendre_values(points, order):
    previous = points * 0.0 + 1.0
    current = points
    for number in range(1, order):
        previous, current = (
            current,
            ((2 * number + 1) * points * current - number * previous) / (number + 1),
        )
    return current


def tables():
    order = NODES - 1
    points = np.concatenate([np.array([-1.0]), np.array(gll_inner), np.array([1.0])])
    values = legendre_values(points, order)
    eye = np.eye(NODES)
    differ = points[:, None] - points[None, :] + eye
    offdiag = np.where(eye > 0, 0.0, values[:, None] / values[None, :] / differ)
    ends = np.concatenate(
        [
            np.array([-order * (order + 1) / 4.0]),
            np.zeros(NODES - 2),
            np.array([order * (order + 1) / 4.0]),
        ]
    )
    derivative = offdiag + eye * ends[None, :]
    linear = np.stack([(1.0 - points) / 2.0, (1.0 + points) / 2.0], axis=1)
    return derivative.astype(np.float32), linear.astype(np.float32)


def halves(matrix):
    matrix = matrix.astype(np.float32)
    high = matrix.astype(jnp.bfloat16)
    low = (matrix - high.astype(np.float32)).astype(jnp.bfloat16)
    return high, low


def left_table(matrix):
    return np.stack(halves(matrix))


def right_table(matrix):
    high, low = halves(matrix)
    return np.block([[high, low], [high, np.zeros_like(low)]])


def split(value):
    high = value.astype(jnp.bfloat16)
    low = (value - high.astype(jnp.float32)).astype(jnp.bfloat16)
    return high, low


def dot(a, b):
    return jnp.dot(a, b, preferred_element_type=jnp.float32)


def left(table, value):
    high, low = split(value)
    n = value.shape[1]
    both = dot(table[0], jnp.concatenate([high, low], axis=1))
    return both[:, :n] + both[:, n:] + dot(table[1], high)


def right(value, table):
    high, low = split(value)
    n = value.shape[1]
    both = dot(jnp.concatenate([high, low], axis=1), table[...])
    return both[:, :n] + both[:, n:]


def three_rows(row):
    high = row.astype(jnp.bfloat16).astype(jnp.float32)
    rest = row - high
    mid = rest.astype(jnp.bfloat16).astype(jnp.float32)
    low = rest - mid
    place = lax.broadcasted_iota(jnp.int32, (8, row.shape[1]), 0)
    zero = jnp.zeros((8, row.shape[1]), jnp.float32)
    return jnp.where(
        place == 0, high, jnp.where(place == 1, mid, jnp.where(place == 2, low, zero))
    ).astype(jnp.bfloat16)


def kernel(
    sizes,
    derivative,
    res_ref,
    geo_ref,
    hel_ref,
    ids_ref,
    cc_ref,
    dy_ref,
    dyt_ref,
    sqy_ref,
    dz_ref,
    dzt_ref,
    sqz_ref,
    pxy_ref,
    pxyt_ref,
    pz_ref,
    out_ref,
    coarse_ref,
    fbuf,
    xs,
    ys,
    xr,
    yr,
    dr,
    onehot,
    csend,
    crecv,
    psend,
    precv,
    send_sem,
    recv_sem,
    csend_sem,
    crecv_sem,
    psend_sem,
    precv_sem,
):
    nw, nn, sx, sy, sz, slots, padded = sizes
    rows = sx * sy
    w, n = lax.axis_index("wide"), lax.axis_index("narrow")
    ez = sz // NODES
    pairs = (sx // NODES) * (sy // NODES)

    def exists(step):
        dw, dn = step
        cond = None
        for place, move, count in ((w, dw, nw), (n, dn, nn)):
            if move:
                here = place > 0 if move < 0 else place < count - 1
                cond = here if cond is None else jnp.logical_and(cond, here)
        return cond

    barrier = pltpu.get_barrier_semaphore()
    for step in DIRS[:6]:

        @pl.when(exists(step))
        def _():
            pl.semaphore_signal(
                barrier, inc=1, device_id=(w + step[0], n + step[1]), device_id_type=MESH
            )

    for j in range(1, nn):
        pl.semaphore_signal(
            barrier, inc=1, device_id=(w, lax.rem(n + j, nn)), device_id_type=MESH
        )

    def barrier_wait():
        peers = nn - 1
        for step in DIRS[:6]:
            peers = peers + jnp.where(exists(step), 1, 0)
        pl.semaphore_wait(barrier, peers)

    def buffers(field, k):
        dw, dn = DIRS[k]
        xside, yside = int(dw > 0), int(dn > 0)
        o = OPPOSITE[k]
        if dn == 0:
            return xs.at[field, xside], xr.at[field, int(DIRS[o][0] > 0)]
        if dw == 0:
            return ys.at[field, yside], yr.at[field, int(DIRS[o][1] > 0)]
        line = sy - 1 if dn > 0 else 0
        return xs.at[field, xside, pl.ds(line, 1)], dr.at[field, o - 2]

    def descriptor(field, k):
        source, target = buffers(field, k)
        return pltpu.make_async_remote_copy(
            src_ref=source,
            dst_ref=target,
            send_sem=send_sem.at[field, k],
            recv_sem=recv_sem.at[field, OPPOSITE[k]],
            device_id=(w + DIRS[k][0], n + DIRS[k][1]),
            device_id_type=MESH,
        )

    lane = lax.broadcasted_iota(jnp.int32, (1, sz), 1)
    z_low = jnp.logical_and(lane % NODES == 0, lane > 0)
    z_high = jnp.logical_and(lane % NODES == NODES - 1, lane < sz - 1)
    sub = lax.broadcasted_iota(jnp.int32, (1, NODES, 1), 1)

    def local_sum(value):
        value = (
            value
            + jnp.where(z_low, pltpu.roll(value, 1, 1), 0.0)
            + jnp.where(z_high, pltpu.roll(value, sz - 1, 1), 0.0)
        )
        cube = value.reshape(sx, sy // NODES, NODES, sz)
        parts = []
        count = sy // NODES
        for e in range(count):
            block = cube[:, e]
            if e > 0:
                block = block + jnp.where(sub == 0, pltpu.roll(cube[:, e - 1], 1, 1), 0.0)
            if e < count - 1:
                block = block + jnp.where(
                    sub == NODES - 1, pltpu.roll(cube[:, e + 1], NODES - 1, 1), 0.0
                )
            parts.append(block)
        cube = jnp.stack(parts, axis=1).reshape(sx, sy, sz)
        planes = []
        for x in range(sx):
            plane = cube[x]
            if x % NODES == 0 and x > 0:
                plane = plane + cube[x - 1]
            if x % NODES == NODES - 1 and x < sx - 1:
                plane = plane + cube[x + 1]
            planes.append(plane)
        return jnp.stack(planes, axis=0).reshape(rows, sz)

    def prepare(field, value):
        value = local_sum(value)
        xs[field, 0] = value[:sy]
        xs[field, 1] = value[rows - sy :]
        fbuf[field] = value
        ys[field, 0] = fbuf[field, pl.ds(0, sx, stride=sy), :]
        ys[field, 1] = fbuf[field, pl.ds(sy - 1, sx, stride=sy), :]

    def send(field):
        for k, step in enumerate(DIRS):

            @pl.when(exists(step))
            def _():
                descriptor(field, k).start()

    def finish(field):
        for k in (6, 7, 0, 1, 2, 3, 4, 5):
            dw, dn = DIRS[k]

            @pl.when(exists(DIRS[k]))
            def _():
                descriptor(field, OPPOSITE[k]).wait_recv()
                first = 0 if dw < 0 else rows - sy
                if dn == 0:
                    fbuf[field, pl.ds(first, sy), :] += xr[field, int(dw > 0)]
                elif dw == 0:
                    line = 0 if dn < 0 else sy - 1
                    fbuf[field, pl.ds(line, sx, stride=sy), :] += yr[field, int(dn > 0)]
                else:
                    line = first + (0 if dn < 0 else sy - 1)
                    fbuf[field, pl.ds(line, 1), :] += dr[field, k - 2]

        return fbuf[field]

    def along_x(value, matrix):
        cube = value.reshape(sx // NODES, NODES, sy, sz)
        out = []
        for a in range(NODES):
            total = None
            for b in range(NODES):
                entry = float(matrix[a, b])
                if entry == 0.0:
                    continue
                term = entry * cube[:, b]
                total = term if total is None else total + term
            out.append(total)
        return jnp.stack(out, axis=1).reshape(rows, sz)

    def element_operator(value):
        gx = along_x(value, derivative) * geo_ref[0]
        gy = left(dy_ref, value) * geo_ref[1]
        gz = right(value, dz_ref) * geo_ref[2]
        return (
            along_x(gx, derivative.T)
            + left(dyt_ref, gy)
            + right(gz, dzt_ref)
            + hel_ref[...] * value
        )

    prepare(RES, res_ref[...])
    square = derivative * derivative
    prepare(
        DIAG,
        along_x(geo_ref[0], square.T)
        + left(sqy_ref, geo_ref[1])
        + right(geo_ref[2], sqz_ref)
        + hel_ref[...],
    )
    csend[...] = cc_ref[...]
    barrier_wait()

    def coarse_copy(source, target, sems, rsems, j):
        peer = lax.rem(n + j, nn)
        return pltpu.make_async_remote_copy(
            src_ref=source,
            dst_ref=target,
            send_sem=sems.at[j],
            recv_sem=rsems.at[j],
            device_id=(w, peer),
            device_id_type=MESH,
        )

    for j in range(1, nn):
        coarse_copy(csend, crecv.at[j], csend_sem, crecv_sem, j).start()
    send(DIAG)
    send(RES)

    lanes = lax.broadcasted_iota(jnp.int32, (1, padded), 1)
    values = []
    for j in range(nn):
        owner = lax.rem(n - j + nn, nn)
        values.append(jnp.where(lanes < slots, owner * slots + lanes, -1))
    numbers = jnp.concatenate(values, axis=1)
    for pair in range(pairs):
        block = ids_ref[pair].T
        for v in range(8):
            onehot[pl.ds((pair * 8 + v) * ez, ez), :] = jnp.where(
                block[:, v : v + 1] == numbers, 1.0, 0.0
            ).astype(jnp.bfloat16)

    pieces = [csend[...]]
    for j in range(1, nn):
        coarse_copy(csend, crecv.at[j], csend_sem, crecv_sem, j).wait_recv()
        pieces.append(crecv[j])
    whole = jnp.concatenate(pieces, axis=1)
    contract_last = (((1,), (1,)), ((), ()))
    picked = jnp.sum(
        lax.dot_general(
            three_rows(whole), onehot[...], contract_last, preferred_element_type=jnp.float32
        ),
        axis=0,
        keepdims=True,
    )
    columns = pairs * 8 * ez
    groups = pairs * 4
    row_of = lax.broadcasted_iota(jnp.int32, (groups, columns), 1) // (2 * ez)
    mine = row_of == lax.broadcasted_iota(jnp.int32, (groups, columns), 0)
    spread = jnp.where(mine, picked, 0.0)
    along_z = jnp.dot(
        spread, pz_ref[...], precision=HIGHEST, preferred_element_type=jnp.float32
    )
    correction = jnp.dot(
        pxy_ref[...], along_z, precision=HIGHEST, preferred_element_type=jnp.float32
    )
    prepare(CORR, element_operator(correction))
    send(CORR)

    inverse = 1.0 / finish(DIAG)
    residual = finish(RES)

    theta = 0.5 * (high_bound + low_bound)
    delta = 0.5 * (high_bound - low_bound)
    sigma = theta / delta

    rho = 1.0 / sigma
    update = inverse * residual * (1.0 / theta)
    solution_value = correction
    for number in range(DEGREE):
        solution_value = solution_value + update
        field = FIRST + number
        prepare(field, element_operator(update))
        send(field)
        residual = residual - finish(field)
        if number + 1 < DEGREE:
            rho_next = 1.0 / (2.0 * sigma - rho)
            update = (rho_next * rho) * update + (2.0 * rho_next / delta) * inverse * residual
            rho = rho_next

    pre_residual = residual
    residual = residual - finish(CORR)
    rho = 1.0 / sigma
    update = inverse * residual * (1.0 / theta)
    for number in range(DEGREE):
        solution_value = solution_value + update
        if number < DEGREE - 1:
            field = FIRST + DEGREE + number
            prepare(field, element_operator(update))
            send(field)
            if number == 0:
                point = lax.broadcasted_iota(jnp.int32, (rows, sz), 0)
                x, y = point // sy, point % sy
                z = lax.broadcasted_iota(jnp.int32, (rows, sz), 1)
                weighted = pre_residual
                for local, start, total in (
                    (x, w * sx, nw * sx),
                    (y, n * sy, nn * sy),
                    (z, 0, sz),
                ):
                    spot = start + local
                    inner = jnp.logical_or(
                        jnp.logical_and(local % NODES == 0, spot > 0),
                        jnp.logical_and(local % NODES == NODES - 1, spot < total - 1),
                    )
                    weighted = weighted * jnp.where(inner, 0.5, 1.0)
                on_xy = jnp.dot(
                    pxyt_ref[...], weighted, precision=HIGHEST, preferred_element_type=jnp.float32
                )
                on_z = lax.dot_general(
                    on_xy,
                    pz_ref[...],
                    contract_last,
                    precision=HIGHEST,
                    preferred_element_type=jnp.float32,
                )
                corners = jnp.sum(jnp.where(mine, on_z, 0.0), axis=0, keepdims=True)
                partial = jnp.sum(dot(three_rows(corners), onehot[...]), axis=0, keepdims=True)
                for j in range(1, nn):
                    at = (nn - j) * padded
                    psend[j] = partial[:, at : at + padded]
                    coarse_copy(psend.at[j], precv.at[j], psend_sem, precv_sem, j).start()
                own = partial[:, :padded]
            residual = residual - finish(field)
            rho_next = 1.0 / (2.0 * sigma - rho)
            update = (rho_next * rho) * update + (2.0 * rho_next / delta) * inverse * residual
            rho = rho_next
    out_ref[...] = solution_value

    for j in range(1, nn):
        coarse_copy(psend.at[j], precv.at[j], psend_sem, precv_sem, j).wait_recv()
        own = own + precv[j]
    coarse_ref[...] = own

    for j in range(1, nn):
        coarse_copy(csend, crecv.at[j], csend_sem, crecv_sem, j).wait_send()
        coarse_copy(psend.at[j], precv.at[j], psend_sem, precv_sem, j).wait_send()
    for field in range(FIELDS):
        for k, step in enumerate(DIRS):

            @pl.when(exists(step))
            def _():
                descriptor(field, k).wait_send()


def on_device(nw, nn, residual_local, geometry, helmholtz, coarse_ids, coarse_correction):
    derivative, linear = tables()
    sx, sy, sz = residual_local.shape
    rows = sx * sy
    slots = coarse_correction.shape[0]
    padded = -(-slots // 128) * 128
    ex, ey, ez = sx // NODES, sy // NODES, sz // NODES
    pairs = ex * ey
    square = derivative * derivative
    eye_y, eye_z = np.eye(rows // NODES), np.eye(ez)

    pxy = np.einsum("eE,ia,fF,jb->eifjEFab", np.eye(ex), linear, np.eye(ey), linear)
    pxy = pxy.reshape(rows, pairs * 4).astype(np.float32)
    pz = np.einsum("kc,eE->cEek", linear, eye_z).reshape(2 * ez, sz)
    pz = np.tile(pz, (pairs * 4, 1)).astype(np.float32)

    constants = (
        left_table(np.kron(eye_y, derivative)),
        left_table(np.kron(eye_y, derivative.T)),
        left_table(np.kron(eye_y, square.T)),
        right_table(np.kron(eye_z, derivative.T)),
        right_table(np.kron(eye_z, derivative)),
        right_table(np.kron(eye_z, square)),
        pxy,
        np.ascontiguousarray(pxy.T),
        pz,
    )
    coarse_row = coarse_correction.reshape(1, slots)
    if padded != slots:
        coarse_row = jnp.pad(coarse_row, ((0, 0), (0, padded - slots)))

    f32 = jnp.float32
    dma = pltpu.SemaphoreType.DMA
    vmem = pl.BlockSpec(memory_space=pltpu.VMEM)
    out, coarse = pl.pallas_call(
        functools.partial(kernel, (nw, nn, sx, sy, sz, slots, padded), derivative),
        out_shape=(
            jax.ShapeDtypeStruct((rows, sz), f32),
            jax.ShapeDtypeStruct((1, padded), f32),
        ),
        in_specs=[vmem] * 14,
        out_specs=(vmem, vmem),
        scratch_shapes=[
            pltpu.VMEM((FIELDS, rows, sz), f32),
            pltpu.VMEM((FIELDS, 2, sy, sz), f32),
            pltpu.VMEM((FIELDS, 2, sx, sz), f32),
            pltpu.VMEM((FIELDS, 2, sy, sz), f32),
            pltpu.VMEM((FIELDS, 2, sx, sz), f32),
            pltpu.VMEM((FIELDS, 4, 1, sz), f32),
            pltpu.VMEM((pairs * 8 * ez, nn * padded), jnp.bfloat16),
            pltpu.VMEM((1, padded), f32),
            pltpu.VMEM((nn, 1, padded), f32),
            pltpu.VMEM((nn, 1, padded), f32),
            pltpu.VMEM((nn, 1, padded), f32),
            dma((FIELDS, len(DIRS))),
            dma((FIELDS, len(DIRS))),
            dma((nn,)),
            dma((nn,)),
            dma((nn,)),
            dma((nn,)),
        ],
        compiler_params=pltpu.CompilerParams(collective_id=0, has_side_effects=True),
    )(
        residual_local.reshape(rows, sz),
        geometry.reshape(3, rows, sz),
        helmholtz.reshape(rows, sz),
        coarse_ids.transpose(0, 1, 3, 2).reshape(pairs, 8, ez),
        coarse_row,
        *[jnp.asarray(c) for c in constants],
    )
    return out.reshape(sx, sy, sz), coarse[:, :slots].reshape(slots)


def solution(mesh):
    return jax.shard_map(
        functools.partial(on_device, mesh.shape["wide"], mesh.shape["narrow"]),
        mesh=mesh,
        in_specs=(
            P("wide", "narrow", None),
            P(None, "wide", "narrow", None),
            P("wide", "narrow", None),
            P("wide", "narrow", None, None),
            P(("wide", "narrow")),
        ),
        out_specs=(P("wide", "narrow", None), P(("wide", "narrow"))),
        check_vma=False,
    )
```

```python
import functools
import math

import jax
import jax.numpy as jnp
import numpy as np
from jax import lax
from jax.experimental import pallas as pl
from jax.experimental.pallas import tpu as pltpu
from jax.sharding import PartitionSpec as P

NODES = 8
DEGREE = 3
MESH = pl.DeviceIdType.MESH
HIGHEST = lax.Precision.HIGHEST

low_bound = 0.3
high_bound = 3.3
gll_inner = (
    -0.8717401485096066,
    -0.5917001814331423,
    -0.2092992179024789,
    0.2092992179024789,
    0.5917001814331423,
    0.8717401485096066,
)

DIRS = ((-1, 0), (1, 0), (-1, -1), (-1, 1), (1, -1), (1, 1), (0, -1), (0, 1))
X_DIRS, Y_DIRS = (0, 1, 2, 3, 4, 5), (6, 7)
OPPOSITE = tuple(DIRS.index((-a, -b)) for a, b in DIRS)

DIAG, RES, CORR, FIRST = 0, 1, 2, 3
FIELDS = FIRST + 2 * DEGREE - 1


def legendre_values(points, order):
    previous = points * 0.0 + 1.0
    current = points
    for number in range(1, order):
        previous, current = (
            current,
            ((2 * number + 1) * points * current - number * previous) / (number + 1),
        )
    return current


def tables():
    order = NODES - 1
    points = np.concatenate([np.array([-1.0]), np.array(gll_inner), np.array([1.0])])
    values = legendre_values(points, order)
    eye = np.eye(NODES)
    differ = points[:, None] - points[None, :] + eye
    offdiag = np.where(eye > 0, 0.0, values[:, None] / values[None, :] / differ)
    ends = np.concatenate(
        [
            np.array([-order * (order + 1) / 4.0]),
            np.zeros(NODES - 2),
            np.array([order * (order + 1) / 4.0]),
        ]
    )
    derivative = offdiag + eye * ends[None, :]
    linear = np.stack([(1.0 - points) / 2.0, (1.0 + points) / 2.0], axis=1)
    return derivative.astype(np.float32), linear.astype(np.float32)


def halves(matrix):
    matrix = matrix.astype(np.float32)
    high = matrix.astype(jnp.bfloat16)
    low = (matrix - high.astype(np.float32)).astype(jnp.bfloat16)
    return high, low


def left_table(matrix):
    return np.stack(halves(matrix))


def right_table(matrix):
    high, low = halves(matrix)
    return np.block([[high, low], [high, np.zeros_like(low)]])


def split(value):
    high = value.astype(jnp.bfloat16)
    low = (value - high.astype(jnp.float32)).astype(jnp.bfloat16)
    return high, low


def dot(a, b):
    return jnp.dot(a, b, preferred_element_type=jnp.float32)


def left(table, value):
    high, low = split(value)
    n = value.shape[1]
    both = dot(table[0], jnp.concatenate([high, low], axis=1))
    return both[:, :n] + both[:, n:] + dot(table[1], high)


def right(value, table):
    high, low = split(value)
    n = value.shape[1]
    both = dot(jnp.concatenate([high, low], axis=1), table[...])
    return both[:, :n] + both[:, n:]


def three_rows(row):
    high = row.astype(jnp.bfloat16).astype(jnp.float32)
    rest = row - high
    mid = rest.astype(jnp.bfloat16).astype(jnp.float32)
    low = rest - mid
    place = lax.broadcasted_iota(jnp.int32, (8, row.shape[1]), 0)
    zero = jnp.zeros((8, row.shape[1]), jnp.float32)
    return jnp.where(
        place == 0, high, jnp.where(place == 1, mid, jnp.where(place == 2, low, zero))
    ).astype(jnp.bfloat16)


def kernel(
    sizes,
    derivative,
    res_ref,
    geo_ref,
    hel_ref,
    ids_ref,
    cc_ref,
    dy_ref,
    dyt_ref,
    sqy_ref,
    dz_ref,
    dzt_ref,
    sqz_ref,
    pxy_ref,
    pxyt_ref,
    pz_ref,
    out_ref,
    coarse_ref,
    fbuf,
    xs,
    ys,
    xr,
    yr,
    dr,
    gm,
    tsend,
    trecv,
    onehot,
    csend,
    crecv,
    psend,
    precv,
    send_sem,
    recv_sem,
    csend_sem,
    crecv_sem,
    psend_sem,
    precv_sem,
    tsend_sem,
    trecv_sem,
):
    nw, nn, sx, sy, sz, slots, padded = sizes
    rows = sx * sy
    w, n = lax.axis_index("wide"), lax.axis_index("narrow")
    ez = sz // NODES
    pairs = (sx // NODES) * (sy // NODES)

    def exists(step):
        dw, dn = step
        cond = None
        for place, move, count in ((w, dw, nw), (n, dn, nn)):
            if move:
                here = place > 0 if move < 0 else place < count - 1
                cond = here if cond is None else jnp.logical_and(cond, here)
        return cond

    barrier = pltpu.get_barrier_semaphore()
    for step in DIRS[:6]:

        @pl.when(exists(step))
        def _():
            pl.semaphore_signal(
                barrier, inc=1, device_id=(w + step[0], n + step[1]), device_id_type=MESH
            )

    for j in range(1, nn):
        pl.semaphore_signal(
            barrier, inc=1, device_id=(w, lax.rem(n + j, nn)), device_id_type=MESH
        )

    def barrier_wait():
        peers = nn - 1
        for step in DIRS[:6]:
            peers = peers + jnp.where(exists(step), 1, 0)
        pl.semaphore_wait(barrier, peers)

    def buffers(field, k):
        dw, dn = DIRS[k]
        xside, yside = int(dw > 0), int(dn > 0)
        o = OPPOSITE[k]
        if dn == 0:
            return xs.at[field, xside], xr.at[field, int(DIRS[o][0] > 0)]
        if dw == 0:
            return ys.at[field, yside], yr.at[field, int(DIRS[o][1] > 0)]
        line = sy - 1 if dn > 0 else 0
        return xs.at[field, xside, pl.ds(line, 1)], dr.at[field, o - 2]

    def descriptor(field, k):
        source, target = buffers(field, k)
        return pltpu.make_async_remote_copy(
            src_ref=source,
            dst_ref=target,
            send_sem=send_sem.at[field, k],
            recv_sem=recv_sem.at[field, OPPOSITE[k]],
            device_id=(w + DIRS[k][0], n + DIRS[k][1]),
            device_id_type=MESH,
        )

    lane = lax.broadcasted_iota(jnp.int32, (1, sz), 1)
    z_low = jnp.logical_and(lane % NODES == 0, lane > 0)
    z_high = jnp.logical_and(lane % NODES == NODES - 1, lane < sz - 1)
    sub = lax.broadcasted_iota(jnp.int32, (1, NODES, 1), 1)

    def sum_yz(value):
        value = (
            value
            + jnp.where(z_low, pltpu.roll(value, 1, 1), 0.0)
            + jnp.where(z_high, pltpu.roll(value, sz - 1, 1), 0.0)
        )
        cube = value.reshape(value.shape[0] // sy, sy // NODES, NODES, sz)
        parts = []
        count = sy // NODES
        for e in range(count):
            block = cube[:, e]
            if e > 0:
                block = block + jnp.where(sub == 0, pltpu.roll(cube[:, e - 1], 1, 1), 0.0)
            if e < count - 1:
                block = block + jnp.where(
                    sub == NODES - 1, pltpu.roll(cube[:, e + 1], NODES - 1, 1), 0.0
                )
            parts.append(block)
        return jnp.stack(parts, axis=1).reshape(value.shape)

    def local_sum(value):
        cube = sum_yz(value).reshape(sx, sy, sz)
        planes = []
        for x in range(sx):
            plane = cube[x]
            if x % NODES == 0 and x > 0:
                plane = plane + cube[x - 1]
            if x % NODES == NODES - 1 and x < sx - 1:
                plane = plane + cube[x + 1]
            planes.append(plane)
        return jnp.stack(planes, axis=0).reshape(rows, sz)

    def prepare(field, value, with_faces):
        value = local_sum(value)
        if with_faces:
            xs[field, 0] = value[:sy]
            xs[field, 1] = value[rows - sy :]
        fbuf[field] = value
        ys[field, 0] = fbuf[field, pl.ds(0, sx, stride=sy), :]
        ys[field, 1] = fbuf[field, pl.ds(sy - 1, sx, stride=sy), :]

    def send(field, ks):
        for k in ks:

            @pl.when(exists(DIRS[k]))
            def _():
                descriptor(field, k).start()

    def finish(field, ks):
        for k in ks:
            dw, dn = DIRS[k]

            @pl.when(exists(DIRS[k]))
            def _():
                descriptor(field, OPPOSITE[k]).wait_recv()
                first = 0 if dw < 0 else rows - sy
                if dn == 0:
                    fbuf[field, pl.ds(first, sy), :] += xr[field, int(dw > 0)]
                elif dw == 0:
                    line = 0 if dn < 0 else sy - 1
                    fbuf[field, pl.ds(line, sx, stride=sy), :] += yr[field, int(dn > 0)]
                else:
                    line = first + (0 if dn < 0 else sy - 1)
                    fbuf[field, pl.ds(line, 1), :] += dr[field, k - 2]

    def patch(value, faces):
        return jnp.concatenate([faces[:sy], value[sy : rows - sy], faces[sy:]], axis=0)

    def faces_of(value):
        return jnp.concatenate([value[:sy], value[rows - sy :]], axis=0)

    def face_part(field):
        return jnp.concatenate(
            [fbuf[field, pl.ds(0, sy), :], fbuf[field, pl.ds(rows - sy, sy), :]], axis=0
        )

    def inner_terms(field, value):
        planes = []
        for base, face in ((0, 0), (sx - NODES, NODES - 1)):
            total = None
            for a in range(NODES):
                inner = None
                for b in range(NODES):
                    entry = float(derivative[a, b])
                    if b == face or entry == 0.0:
                        continue
                    term = entry * value[(base + b) * sy : (base + b + 1) * sy]
                    inner = term if inner is None else inner + term
                entry = float(derivative[a, face])
                if inner is None or entry == 0.0:
                    continue
                term = entry * geo_ref[0, pl.ds((base + a) * sy, sy), :] * inner
                total = term if total is None else total + term
            planes.append(total)
        both = sum_yz(jnp.concatenate(planes, axis=0))
        xs[field, 0] = both[:sy]
        xs[field, 1] = both[sy:]
        send(field, X_DIRS)

    def table_copy(k):
        o = OPPOSITE[k]
        return pltpu.make_async_remote_copy(
            src_ref=tsend.at[k],
            dst_ref=trecv.at[o],
            send_sem=tsend_sem.at[k],
            recv_sem=trecv_sem.at[o],
            device_id=(w + DIRS[k][0], n),
            device_id_type=MESH,
        )

    def along_x(value, matrix):
        cube = value.reshape(sx // NODES, NODES, sy, sz)
        out = []
        for a in range(NODES):
            total = None
            for b in range(NODES):
                entry = float(matrix[a, b])
                if entry == 0.0:
                    continue
                term = entry * cube[:, b]
                total = term if total is None else total + term
            out.append(total)
        return jnp.stack(out, axis=1).reshape(rows, sz)

    def element_operator(value, second, third, mass):
        gx = along_x(value, derivative) * geo_ref[0]
        gy = left(dy_ref, value) * second[...]
        gz = right(value, dz_ref) * third[...]
        return (
            along_x(gx, derivative.T)
            + left(dyt_ref, gy)
            + right(gz, dzt_ref)
            + mass[...] * value
        )

    def with_neighbours(value):
        return element_operator(value, gm.at[0], gm.at[1], gm.at[2])

    prepare(RES, res_ref[...], True)
    square = derivative * derivative
    diagonal_x = along_x(geo_ref[0], square.T)
    for side, first in ((0, 0), (1, rows - sy)):
        tsend[side, 0] = geo_ref[1, pl.ds(first, sy), :]
        tsend[side, 1] = geo_ref[2, pl.ds(first, sy), :]
        tsend[side, 2] = diagonal_x[first : first + sy] + hel_ref[pl.ds(first, sy), :]
    prepare(
        DIAG,
        diagonal_x + left(sqy_ref, geo_ref[1]) + right(geo_ref[2], sqz_ref) + hel_ref[...],
        True,
    )
    csend[...] = cc_ref[...]
    lanes = lax.broadcasted_iota(jnp.int32, (1, padded), 1)
    values = []
    for j in range(nn):
        owner = lax.rem(n - j + nn, nn)
        values.append(jnp.where(lanes < slots, owner * slots + lanes, -1))
    numbers = jnp.concatenate(values, axis=1)
    for pair in range(pairs):
        block = ids_ref[pair].T
        for v in range(8):
            onehot[pl.ds((pair * 8 + v) * ez, ez), :] = jnp.where(
                block[:, v : v + 1] == numbers, 1.0, 0.0
            ).astype(jnp.bfloat16)

    barrier_wait()

    def coarse_copy(source, target, sems, rsems, j):
        peer = lax.rem(n + j, nn)
        return pltpu.make_async_remote_copy(
            src_ref=source,
            dst_ref=target,
            send_sem=sems.at[j],
            recv_sem=rsems.at[j],
            device_id=(w, peer),
            device_id_type=MESH,
        )

    for j in range(1, nn):
        coarse_copy(csend, crecv.at[j], csend_sem, crecv_sem, j).start()
    send(DIAG, Y_DIRS)
    send(RES, Y_DIRS)
    send(DIAG, X_DIRS)
    send(RES, X_DIRS)
    for k in (0, 1):

        @pl.when(exists(DIRS[k]))
        def _():
            table_copy(k).start()

    theta = 0.5 * (high_bound + low_bound)
    delta = 0.5 * (high_bound - low_bound)
    sigma = theta / delta

    finish(DIAG, Y_DIRS)
    finish(RES, Y_DIRS)
    inverse = 1.0 / fbuf[DIAG]
    residual = fbuf[RES]
    update = inverse * residual * (1.0 / theta)
    inner_terms(FIRST, update)

    pieces = [csend[...]]
    for j in range(1, nn):
        coarse_copy(csend, crecv.at[j], csend_sem, crecv_sem, j).wait_recv()
        pieces.append(crecv[j])
    whole = jnp.concatenate(pieces, axis=1)
    contract_last = (((1,), (1,)), ((), ()))
    picked = jnp.sum(
        lax.dot_general(
            three_rows(whole), onehot[...], contract_last, preferred_element_type=jnp.float32
        ),
        axis=0,
        keepdims=True,
    )
    columns = pairs * 8 * ez
    groups = pairs * 4
    row_of = lax.broadcasted_iota(jnp.int32, (groups, columns), 1) // (2 * ez)
    mine = row_of == lax.broadcasted_iota(jnp.int32, (groups, columns), 0)
    spread = jnp.where(mine, picked, 0.0)
    along_z = jnp.dot(
        spread, pz_ref[...], precision=HIGHEST, preferred_element_type=jnp.float32
    )
    correction = jnp.dot(
        pxy_ref[...], along_z, precision=HIGHEST, preferred_element_type=jnp.float32
    )
    prepare(CORR, element_operator(correction, geo_ref.at[1], geo_ref.at[2], hel_ref), True)
    send(CORR, (*Y_DIRS, *X_DIRS))

    gm[0] = geo_ref[1]
    gm[1] = geo_ref[2]
    gm[2] = hel_ref[...]
    for k, first in ((0, 0), (1, rows - sy)):

        @pl.when(exists(DIRS[k]))
        def _():
            table_copy(OPPOSITE[k]).wait_recv()
            for part in range(3):
                gm[part, pl.ds(first, sy), :] += trecv[k, part]

    finish(DIAG, X_DIRS)
    finish(RES, X_DIRS)
    inverse_faces = 1.0 / face_part(DIAG)
    residual_faces = face_part(RES)
    inverse = patch(inverse, inverse_faces)
    residual = patch(residual, residual_faces)
    update = patch(update, inverse_faces * residual_faces * (1.0 / theta))

    rho = 1.0 / sigma
    solution_value = correction
    count = 2 * DEGREE - 1
    for number in range(count):
        solution_value = solution_value + update
        field = FIRST + number
        prepare(field, with_neighbours(update), False)
        send(field, Y_DIRS)
        if number == DEGREE - 1:
            finish(CORR, (*Y_DIRS, *X_DIRS))
        finish(field, Y_DIRS)

        old_residual, old_update = residual, update
        residual = old_residual - fbuf[field]
        if number == DEGREE - 1:
            image = fbuf[CORR]
            shifted = residual - image
            update = inverse * shifted * (1.0 / theta)
        else:
            rho_next = 1.0 / (2.0 * sigma - rho)
            keep, gain = rho_next * rho, 2.0 * rho_next / delta
            rho = rho_next
            update = keep * old_update + gain * inverse * residual
        if number + 1 < count:
            inner_terms(field + 1, update)
        if number == DEGREE:
            point = lax.broadcasted_iota(jnp.int32, (rows, sz), 0)
            x, y = point // sy, point % sy
            z = lax.broadcasted_iota(jnp.int32, (rows, sz), 1)
            weighted = pre_residual
            for local, start, total in (
                (x, w * sx, nw * sx),
                (y, n * sy, nn * sy),
                (z, 0, sz),
            ):
                spot = start + local
                inner = jnp.logical_or(
                    jnp.logical_and(local % NODES == 0, spot > 0),
                    jnp.logical_and(local % NODES == NODES - 1, spot < total - 1),
                )
                weighted = weighted * jnp.where(inner, 0.5, 1.0)
            on_xy = jnp.dot(
                pxyt_ref[...], weighted, precision=HIGHEST, preferred_element_type=jnp.float32
            )
            on_z = lax.dot_general(
                on_xy,
                pz_ref[...],
                contract_last,
                precision=HIGHEST,
                preferred_element_type=jnp.float32,
            )
            corners = jnp.sum(jnp.where(mine, on_z, 0.0), axis=0, keepdims=True)
            partial = jnp.sum(dot(three_rows(corners), onehot[...]), axis=0, keepdims=True)
            for j in range(1, nn):
                at = (nn - j) * padded
                psend[j] = partial[:, at : at + padded]
                coarse_copy(psend.at[j], precv.at[j], psend_sem, precv_sem, j).start()
            own = partial[:, :padded]
        finish(field, X_DIRS)
        residual_faces = faces_of(old_residual) - face_part(field)
        residual = patch(residual, residual_faces)
        if number == DEGREE - 1:
            pre_residual = residual
            shifted_faces = residual_faces - faces_of(image)
            residual = patch(shifted, shifted_faces)
            update = patch(update, inverse_faces * shifted_faces * (1.0 / theta))
            rho = 1.0 / sigma
        else:
            update = patch(
                update, keep * faces_of(old_update) + gain * inverse_faces * residual_faces
            )
    solution_value = solution_value + update
    out_ref[...] = solution_value

    for j in range(1, nn):
        coarse_copy(psend.at[j], precv.at[j], psend_sem, precv_sem, j).wait_recv()
        own = own + precv[j]
    coarse_ref[...] = own

    for j in range(1, nn):
        coarse_copy(csend, crecv.at[j], csend_sem, crecv_sem, j).wait_send()
        coarse_copy(psend.at[j], precv.at[j], psend_sem, precv_sem, j).wait_send()
    for field in range(FIELDS):
        for k, step in enumerate(DIRS):

            @pl.when(exists(step))
            def _():
                descriptor(field, k).wait_send()

    for k in (0, 1):

        @pl.when(exists(DIRS[k]))
        def _():
            table_copy(k).wait_send()


def on_device(nw, nn, residual_local, geometry, helmholtz, coarse_ids, coarse_correction):
    derivative, linear = tables()
    sx, sy, sz = residual_local.shape
    rows = sx * sy
    slots = coarse_correction.shape[0]
    padded = -(-slots // 128) * 128
    ex, ey, ez = sx // NODES, sy // NODES, sz // NODES
    pairs = ex * ey
    square = derivative * derivative
    eye_y, eye_z = np.eye(rows // NODES), np.eye(ez)

    pxy = np.einsum("eE,ia,fF,jb->eifjEFab", np.eye(ex), linear, np.eye(ey), linear)
    pxy = pxy.reshape(rows, pairs * 4).astype(np.float32)
    pz = np.einsum("kc,eE->cEek", linear, eye_z).reshape(2 * ez, sz)
    pz = np.tile(pz, (pairs * 4, 1)).astype(np.float32)

    constants = (
        left_table(np.kron(eye_y, derivative)),
        left_table(np.kron(eye_y, derivative.T)),
        left_table(np.kron(eye_y, square.T)),
        right_table(np.kron(eye_z, derivative.T)),
        right_table(np.kron(eye_z, derivative)),
        right_table(np.kron(eye_z, square)),
        pxy,
        np.ascontiguousarray(pxy.T),
        pz,
    )
    coarse_row = coarse_correction.reshape(1, slots)
    if padded != slots:
        coarse_row = jnp.pad(coarse_row, ((0, 0), (0, padded - slots)))

    f32 = jnp.float32
    dma = pltpu.SemaphoreType.DMA
    vmem = pl.BlockSpec(memory_space=pltpu.VMEM)
    out, coarse = pl.pallas_call(
        functools.partial(kernel, (nw, nn, sx, sy, sz, slots, padded), derivative),
        out_shape=(
            jax.ShapeDtypeStruct((rows, sz), f32),
            jax.ShapeDtypeStruct((1, padded), f32),
        ),
        in_specs=[vmem] * 14,
        out_specs=(vmem, vmem),
        scratch_shapes=[
            pltpu.VMEM((FIELDS, rows, sz), f32),
            pltpu.VMEM((FIELDS, 2, sy, sz), f32),
            pltpu.VMEM((FIELDS, 2, sx, sz), f32),
            pltpu.VMEM((FIELDS, 2, sy, sz), f32),
            pltpu.VMEM((FIELDS, 2, sx, sz), f32),
            pltpu.VMEM((FIELDS, 4, 1, sz), f32),
            pltpu.VMEM((3, rows, sz), f32),
            pltpu.VMEM((2, 3, sy, sz), f32),
            pltpu.VMEM((2, 3, sy, sz), f32),
            pltpu.VMEM((pairs * 8 * ez, nn * padded), jnp.bfloat16),
            pltpu.VMEM((1, padded), f32),
            pltpu.VMEM((nn, 1, padded), f32),
            pltpu.VMEM((nn, 1, padded), f32),
            pltpu.VMEM((nn, 1, padded), f32),
            dma((FIELDS, len(DIRS))),
            dma((FIELDS, len(DIRS))),
            dma((nn,)),
            dma((nn,)),
            dma((nn,)),
            dma((nn,)),
            dma((2,)),
            dma((2,)),
        ],
        compiler_params=pltpu.CompilerParams(collective_id=0, has_side_effects=True),
    )(
        residual_local.reshape(rows, sz),
        geometry.reshape(3, rows, sz),
        helmholtz.reshape(rows, sz),
        coarse_ids.transpose(0, 1, 3, 2).reshape(pairs, 8, ez),
        coarse_row,
        *[jnp.asarray(c) for c in constants],
    )
    return out.reshape(sx, sy, sz), coarse[:, :slots].reshape(slots)


def solution(mesh):
    return jax.shard_map(
        functools.partial(on_device, mesh.shape["wide"], mesh.shape["narrow"]),
        mesh=mesh,
        in_specs=(
            P("wide", "narrow", None),
            P(None, "wide", "narrow", None),
            P("wide", "narrow", None),
            P("wide", "narrow", None, None),
            P(("wide", "narrow")),
        ),
        out_specs=(P("wide", "narrow", None), P(("wide", "narrow"))),
        check_vma=False,
    )
```

```python
import functools
import math

import jax
import jax.numpy as jnp
import numpy as np
from jax import lax
from jax.experimental import pallas as pl
from jax.experimental.pallas import tpu as pltpu
from jax.sharding import PartitionSpec as P

NODES = 8
DEGREE = 3
MESH = pl.DeviceIdType.MESH
HIGHEST = lax.Precision.HIGHEST

low_bound = 0.3
high_bound = 3.3
gll_inner = (
    -0.8717401485096066,
    -0.5917001814331423,
    -0.2092992179024789,
    0.2092992179024789,
    0.5917001814331423,
    0.8717401485096066,
)

DIRS = ((-1, 0), (1, 0), (-1, -1), (-1, 1), (1, -1), (1, 1), (0, -1), (0, 1))
X_DIRS, Y_DIRS = (0, 1, 2, 3, 4, 5), (6, 7)
OPPOSITE = tuple(DIRS.index((-a, -b)) for a, b in DIRS)

DIAG, RES, CORR, FIRST = 0, 1, 2, 3
FIELDS = FIRST + 2 * DEGREE - 1


def legendre_values(points, order):
    previous = points * 0.0 + 1.0
    current = points
    for number in range(1, order):
        previous, current = (
            current,
            ((2 * number + 1) * points * current - number * previous) / (number + 1),
        )
    return current


def tables():
    order = NODES - 1
    points = np.concatenate([np.array([-1.0]), np.array(gll_inner), np.array([1.0])])
    values = legendre_values(points, order)
    eye = np.eye(NODES)
    differ = points[:, None] - points[None, :] + eye
    offdiag = np.where(eye > 0, 0.0, values[:, None] / values[None, :] / differ)
    ends = np.concatenate(
        [
            np.array([-order * (order + 1) / 4.0]),
            np.zeros(NODES - 2),
            np.array([order * (order + 1) / 4.0]),
        ]
    )
    derivative = offdiag + eye * ends[None, :]
    linear = np.stack([(1.0 - points) / 2.0, (1.0 + points) / 2.0], axis=1)
    return derivative.astype(np.float32), linear.astype(np.float32)


def halves(matrix):
    matrix = matrix.astype(np.float32)
    high = matrix.astype(jnp.bfloat16)
    low = (matrix - high.astype(np.float32)).astype(jnp.bfloat16)
    return high, low


def left_table(matrix):
    return np.stack(halves(matrix))


def right_table(matrix):
    high, low = halves(matrix)
    return np.block([[high, low], [high, np.zeros_like(low)]])


def split(value):
    high = value.astype(jnp.bfloat16)
    low = (value - high.astype(jnp.float32)).astype(jnp.bfloat16)
    return high, low


def dot(a, b):
    return jnp.dot(a, b, preferred_element_type=jnp.float32)


def left(table, value):
    high, low = split(value)
    n = value.shape[1]
    both = dot(table[0], jnp.concatenate([high, low], axis=1))
    return both[:, :n] + both[:, n:] + dot(table[1], high)


def right(value, table):
    high, low = split(value)
    n = value.shape[1]
    both = dot(jnp.concatenate([high, low], axis=1), table[...])
    return both[:, :n] + both[:, n:]


ORDER = ("hel", "res", "geo", "sqz", "sqy", "ids", "pz", "pxy", "dz", "dy", "dzt", "dyt", "pxyt")


def three_rows(row):
    high = row.astype(jnp.bfloat16).astype(jnp.float32)
    rest = row - high
    mid = rest.astype(jnp.bfloat16).astype(jnp.float32)
    low = rest - mid
    place = lax.broadcasted_iota(jnp.int32, (8, row.shape[1]), 0)
    zero = jnp.zeros((8, row.shape[1]), jnp.float32)
    return jnp.where(
        place == 0, high, jnp.where(place == 1, mid, jnp.where(place == 2, low, zero))
    ).astype(jnp.bfloat16)


def kernel(
    sizes,
    derivative,
    cc_ref,
    *refs,
):
    count = len(ORDER)
    outside, (out_ref, coarse_ref), inside = refs[:count], refs[count : count + 2], refs[count + 2 :]
    body(sizes, derivative, outside, cc_ref, out_ref, coarse_ref, inside[:count], *inside[count:])


def body(
    sizes,
    derivative,
    outside,
    cc_ref,
    out_ref,
    coarse_ref,
    inside,
    load_sem,
    fbuf,
    xs,
    ys,
    xr,
    yr,
    dr,
    gm,
    tsend,
    trecv,
    onehot,
    csend,
    crecv,
    psend,
    precv,
    send_sem,
    recv_sem,
    csend_sem,
    crecv_sem,
    psend_sem,
    precv_sem,
    tsend_sem,
    trecv_sem,
):
    nw, nn, sx, sy, sz, slots, padded = sizes
    rows = sx * sy
    w, n = lax.axis_index("wide"), lax.axis_index("narrow")
    ez = sz // NODES
    pairs = (sx // NODES) * (sy // NODES)

    def exists(step):
        dw, dn = step
        cond = None
        for place, move, count in ((w, dw, nw), (n, dn, nn)):
            if move:
                here = place > 0 if move < 0 else place < count - 1
                cond = here if cond is None else jnp.logical_and(cond, here)
        return cond

    loads = {
        name: pltpu.make_async_copy(outside[i], inside[i], load_sem.at[i])
        for i, name in enumerate(ORDER)
    }
    at = dict(zip(ORDER, inside))
    res_ref, geo_ref, hel_ref, ids_ref = at["res"], at["geo"], at["hel"], at["ids"]
    dy_ref, dyt_ref, sqy_ref = at["dy"], at["dyt"], at["sqy"]
    dz_ref, dzt_ref, sqz_ref = at["dz"], at["dzt"], at["sqz"]
    pxy_ref, pxyt_ref, pz_ref = at["pxy"], at["pxyt"], at["pz"]

    def loaded(*names):
        for name in names:
            loads[name].wait()

    barrier = pltpu.get_barrier_semaphore()
    for step in DIRS[:6]:

        @pl.when(exists(step))
        def _():
            pl.semaphore_signal(
                barrier, inc=1, device_id=(w + step[0], n + step[1]), device_id_type=MESH
            )

    for j in range(1, nn):
        pl.semaphore_signal(
            barrier, inc=1, device_id=(w, lax.rem(n + j, nn)), device_id_type=MESH
        )

    for name in ORDER:
        loads[name].start()

    def barrier_wait():
        peers = nn - 1
        for step in DIRS[:6]:
            peers = peers + jnp.where(exists(step), 1, 0)
        pl.semaphore_wait(barrier, peers)

    def buffers(field, k):
        dw, dn = DIRS[k]
        xside, yside = int(dw > 0), int(dn > 0)
        o = OPPOSITE[k]
        if dn == 0:
            return xs.at[field, xside], xr.at[field, int(DIRS[o][0] > 0)]
        if dw == 0:
            return ys.at[field, yside], yr.at[field, int(DIRS[o][1] > 0)]
        line = sy - 1 if dn > 0 else 0
        return xs.at[field, xside, pl.ds(line, 1)], dr.at[field, o - 2]

    def descriptor(field, k):
        source, target = buffers(field, k)
        return pltpu.make_async_remote_copy(
            src_ref=source,
            dst_ref=target,
            send_sem=send_sem.at[field, k],
            recv_sem=recv_sem.at[field, OPPOSITE[k]],
            device_id=(w + DIRS[k][0], n + DIRS[k][1]),
            device_id_type=MESH,
        )

    lane = lax.broadcasted_iota(jnp.int32, (1, sz), 1)
    z_low = jnp.logical_and(lane % NODES == 0, lane > 0)
    z_high = jnp.logical_and(lane % NODES == NODES - 1, lane < sz - 1)
    sub = lax.broadcasted_iota(jnp.int32, (1, NODES, 1), 1)

    def sum_yz(value):
        value = (
            value
            + jnp.where(z_low, pltpu.roll(value, 1, 1), 0.0)
            + jnp.where(z_high, pltpu.roll(value, sz - 1, 1), 0.0)
        )
        cube = value.reshape(value.shape[0] // sy, sy // NODES, NODES, sz)
        parts = []
        count = sy // NODES
        for e in range(count):
            block = cube[:, e]
            if e > 0:
                block = block + jnp.where(sub == 0, pltpu.roll(cube[:, e - 1], 1, 1), 0.0)
            if e < count - 1:
                block = block + jnp.where(
                    sub == NODES - 1, pltpu.roll(cube[:, e + 1], NODES - 1, 1), 0.0
                )
            parts.append(block)
        return jnp.stack(parts, axis=1).reshape(value.shape)

    def local_sum(value):
        cube = sum_yz(value).reshape(sx, sy, sz)
        planes = []
        for x in range(sx):
            plane = cube[x]
            if x % NODES == 0 and x > 0:
                plane = plane + cube[x - 1]
            if x % NODES == NODES - 1 and x < sx - 1:
                plane = plane + cube[x + 1]
            planes.append(plane)
        return jnp.stack(planes, axis=0).reshape(rows, sz)

    def prepare(field, value, with_faces):
        value = local_sum(value)
        if with_faces:
            xs[field, 0] = value[:sy]
            xs[field, 1] = value[rows - sy :]
        fbuf[field] = value
        ys[field, 0] = fbuf[field, pl.ds(0, sx, stride=sy), :]
        ys[field, 1] = fbuf[field, pl.ds(sy - 1, sx, stride=sy), :]

    def send(field, ks):
        for k in ks:

            @pl.when(exists(DIRS[k]))
            def _():
                descriptor(field, k).start()

    def finish(field, ks):
        for k in ks:
            dw, dn = DIRS[k]

            @pl.when(exists(DIRS[k]))
            def _():
                descriptor(field, OPPOSITE[k]).wait_recv()
                first = 0 if dw < 0 else rows - sy
                if dn == 0:
                    fbuf[field, pl.ds(first, sy), :] += xr[field, int(dw > 0)]
                elif dw == 0:
                    line = 0 if dn < 0 else sy - 1
                    fbuf[field, pl.ds(line, sx, stride=sy), :] += yr[field, int(dn > 0)]
                else:
                    line = first + (0 if dn < 0 else sy - 1)
                    fbuf[field, pl.ds(line, 1), :] += dr[field, k - 2]

    def patch(value, faces):
        return jnp.concatenate([faces[:sy], value[sy : rows - sy], faces[sy:]], axis=0)

    def faces_of(value):
        return jnp.concatenate([value[:sy], value[rows - sy :]], axis=0)

    def face_part(field):
        return jnp.concatenate(
            [fbuf[field, pl.ds(0, sy), :], fbuf[field, pl.ds(rows - sy, sy), :]], axis=0
        )

    def inner_terms(field, value):
        planes = []
        for base, face in ((0, 0), (sx - NODES, NODES - 1)):
            total = None
            for a in range(NODES):
                inner = None
                for b in range(NODES):
                    entry = float(derivative[a, b])
                    if b == face or entry == 0.0:
                        continue
                    term = entry * value[(base + b) * sy : (base + b + 1) * sy]
                    inner = term if inner is None else inner + term
                entry = float(derivative[a, face])
                if inner is None or entry == 0.0:
                    continue
                term = entry * geo_ref[0, pl.ds((base + a) * sy, sy), :] * inner
                total = term if total is None else total + term
            planes.append(total)
        both = sum_yz(jnp.concatenate(planes, axis=0))
        xs[field, 0] = both[:sy]
        xs[field, 1] = both[sy:]
        send(field, X_DIRS)

    def table_copy(k):
        o = OPPOSITE[k]
        return pltpu.make_async_remote_copy(
            src_ref=tsend.at[k],
            dst_ref=trecv.at[o],
            send_sem=tsend_sem.at[k],
            recv_sem=trecv_sem.at[o],
            device_id=(w + DIRS[k][0], n),
            device_id_type=MESH,
        )

    def along_x(value, matrix):
        cube = value.reshape(sx // NODES, NODES, sy, sz)
        out = []
        for a in range(NODES):
            total = None
            for b in range(NODES):
                entry = float(matrix[a, b])
                if entry == 0.0:
                    continue
                term = entry * cube[:, b]
                total = term if total is None else total + term
            out.append(total)
        return jnp.stack(out, axis=1).reshape(rows, sz)

    def element_operator(value, second, third, mass):
        gx = along_x(value, derivative) * geo_ref[0]
        gy = left(dy_ref, value) * second[...]
        gz = right(value, dz_ref) * third[...]
        return (
            along_x(gx, derivative.T)
            + left(dyt_ref, gy)
            + right(gz, dzt_ref)
            + mass[...] * value
        )

    def with_neighbours(value):
        return element_operator(value, gm.at[0], gm.at[1], gm.at[2])

    loaded("hel", "res")
    prepare(RES, res_ref[...], True)
    loaded("geo", "sqz", "sqy")
    square = derivative * derivative
    diagonal_x = along_x(geo_ref[0], square.T)
    for side, first in ((0, 0), (1, rows - sy)):
        tsend[side, 0] = geo_ref[1, pl.ds(first, sy), :]
        tsend[side, 1] = geo_ref[2, pl.ds(first, sy), :]
        tsend[side, 2] = diagonal_x[first : first + sy] + hel_ref[pl.ds(first, sy), :]
    prepare(
        DIAG,
        diagonal_x + left(sqy_ref, geo_ref[1]) + right(geo_ref[2], sqz_ref) + hel_ref[...],
        True,
    )
    csend[...] = cc_ref[...]
    lanes = lax.broadcasted_iota(jnp.int32, (1, padded), 1)
    values = []
    for j in range(nn):
        owner = lax.rem(n - j + nn, nn)
        values.append(jnp.where(lanes < slots, owner * slots + lanes, -1))
    numbers = jnp.concatenate(values, axis=1)
    loaded("ids")
    for pair in range(pairs):
        block = ids_ref[pair].T
        for v in range(8):
            onehot[pl.ds((pair * 8 + v) * ez, ez), :] = jnp.where(
                block[:, v : v + 1] == numbers, 1.0, 0.0
            ).astype(jnp.bfloat16)

    barrier_wait()

    def coarse_copy(source, target, sems, rsems, j):
        peer = lax.rem(n + j, nn)
        return pltpu.make_async_remote_copy(
            src_ref=source,
            dst_ref=target,
            send_sem=sems.at[j],
            recv_sem=rsems.at[j],
            device_id=(w, peer),
            device_id_type=MESH,
        )

    for j in range(1, nn):
        coarse_copy(csend, crecv.at[j], csend_sem, crecv_sem, j).start()
    send(DIAG, Y_DIRS)
    send(RES, Y_DIRS)
    send(DIAG, X_DIRS)
    send(RES, X_DIRS)
    for k in (0, 1):

        @pl.when(exists(DIRS[k]))
        def _():
            table_copy(k).start()

    theta = 0.5 * (high_bound + low_bound)
    delta = 0.5 * (high_bound - low_bound)
    sigma = theta / delta

    finish(DIAG, Y_DIRS)
    finish(RES, Y_DIRS)
    inverse = 1.0 / fbuf[DIAG]
    residual = fbuf[RES]
    update = inverse * residual * (1.0 / theta)
    inner_terms(FIRST, update)

    loaded("pz", "pxy", "dz", "dy", "dzt", "dyt", "pxyt")
    pieces = [csend[...]]
    for j in range(1, nn):
        coarse_copy(csend, crecv.at[j], csend_sem, crecv_sem, j).wait_recv()
        pieces.append(crecv[j])
    whole = jnp.concatenate(pieces, axis=1)
    contract_last = (((1,), (1,)), ((), ()))
    picked = jnp.sum(
        lax.dot_general(
            three_rows(whole), onehot[...], contract_last, preferred_element_type=jnp.float32
        ),
        axis=0,
        keepdims=True,
    )
    columns = pairs * 8 * ez
    groups = pairs * 4
    row_of = lax.broadcasted_iota(jnp.int32, (groups, columns), 1) // (2 * ez)
    mine = row_of == lax.broadcasted_iota(jnp.int32, (groups, columns), 0)
    spread = jnp.where(mine, picked, 0.0)
    along_z = jnp.dot(
        spread, pz_ref[...], precision=HIGHEST, preferred_element_type=jnp.float32
    )
    correction = jnp.dot(
        pxy_ref[...], along_z, precision=HIGHEST, preferred_element_type=jnp.float32
    )
    prepare(CORR, element_operator(correction, geo_ref.at[1], geo_ref.at[2], hel_ref), True)
    send(CORR, (*Y_DIRS, *X_DIRS))

    gm[0] = geo_ref[1]
    gm[1] = geo_ref[2]
    gm[2] = hel_ref[...]
    for k, first in ((0, 0), (1, rows - sy)):

        @pl.when(exists(DIRS[k]))
        def _():
            table_copy(OPPOSITE[k]).wait_recv()
            for part in range(3):
                gm[part, pl.ds(first, sy), :] += trecv[k, part]

    finish(DIAG, X_DIRS)
    finish(RES, X_DIRS)
    inverse_faces = 1.0 / face_part(DIAG)
    residual_faces = face_part(RES)
    inverse = patch(inverse, inverse_faces)
    residual = patch(residual, residual_faces)
    update = patch(update, inverse_faces * residual_faces * (1.0 / theta))

    rho = 1.0 / sigma
    solution_value = correction
    count = 2 * DEGREE - 1
    for number in range(count):
        solution_value = solution_value + update
        field = FIRST + number
        prepare(field, with_neighbours(update), False)
        send(field, Y_DIRS)
        if number == DEGREE - 1:
            finish(CORR, (*Y_DIRS, *X_DIRS))
        finish(field, Y_DIRS)

        old_residual, old_update = residual, update
        residual = old_residual - fbuf[field]
        if number == DEGREE - 1:
            image = fbuf[CORR]
            shifted = residual - image
            update = inverse * shifted * (1.0 / theta)
        else:
            rho_next = 1.0 / (2.0 * sigma - rho)
            keep, gain = rho_next * rho, 2.0 * rho_next / delta
            rho = rho_next
            update = keep * old_update + gain * inverse * residual
        if number + 1 < count:
            inner_terms(field + 1, update)
        if number == DEGREE:
            point = lax.broadcasted_iota(jnp.int32, (rows, sz), 0)
            x, y = point // sy, point % sy
            z = lax.broadcasted_iota(jnp.int32, (rows, sz), 1)
            weighted = pre_residual
            for local, start, total in (
                (x, w * sx, nw * sx),
                (y, n * sy, nn * sy),
                (z, 0, sz),
            ):
                spot = start + local
                inner = jnp.logical_or(
                    jnp.logical_and(local % NODES == 0, spot > 0),
                    jnp.logical_and(local % NODES == NODES - 1, spot < total - 1),
                )
                weighted = weighted * jnp.where(inner, 0.5, 1.0)
            on_xy = jnp.dot(
                pxyt_ref[...], weighted, precision=HIGHEST, preferred_element_type=jnp.float32
            )
            on_z = lax.dot_general(
                on_xy,
                pz_ref[...],
                contract_last,
                precision=HIGHEST,
                preferred_element_type=jnp.float32,
            )
            corners = jnp.sum(jnp.where(mine, on_z, 0.0), axis=0, keepdims=True)
            partial = jnp.sum(dot(three_rows(corners), onehot[...]), axis=0, keepdims=True)
            for j in range(1, nn):
                at = (nn - j) * padded
                psend[j] = partial[:, at : at + padded]
                coarse_copy(psend.at[j], precv.at[j], psend_sem, precv_sem, j).start()
            own = partial[:, :padded]
        finish(field, X_DIRS)
        residual_faces = faces_of(old_residual) - face_part(field)
        residual = patch(residual, residual_faces)
        if number == DEGREE - 1:
            pre_residual = residual
            shifted_faces = residual_faces - faces_of(image)
            residual = patch(shifted, shifted_faces)
            update = patch(update, inverse_faces * shifted_faces * (1.0 / theta))
            rho = 1.0 / sigma
        else:
            update = patch(
                update, keep * faces_of(old_update) + gain * inverse_faces * residual_faces
            )
    solution_value = solution_value + update
    out_ref[...] = solution_value

    for j in range(1, nn):
        coarse_copy(psend.at[j], precv.at[j], psend_sem, precv_sem, j).wait_recv()
        own = own + precv[j]
    coarse_ref[...] = own

    for j in range(1, nn):
        coarse_copy(csend, crecv.at[j], csend_sem, crecv_sem, j).wait_send()
        coarse_copy(psend.at[j], precv.at[j], psend_sem, precv_sem, j).wait_send()
    for field in range(FIELDS):
        for k, step in enumerate(DIRS):

            @pl.when(exists(step))
            def _():
                descriptor(field, k).wait_send()

    for k in (0, 1):

        @pl.when(exists(DIRS[k]))
        def _():
            table_copy(k).wait_send()


def on_device(nw, nn, residual_local, geometry, helmholtz, coarse_ids, coarse_correction):
    derivative, linear = tables()
    sx, sy, sz = residual_local.shape
    rows = sx * sy
    slots = coarse_correction.shape[0]
    padded = -(-slots // 128) * 128
    ex, ey, ez = sx // NODES, sy // NODES, sz // NODES
    pairs = ex * ey
    square = derivative * derivative
    eye_y, eye_z = np.eye(rows // NODES), np.eye(ez)

    pxy = np.einsum("eE,ia,fF,jb->eifjEFab", np.eye(ex), linear, np.eye(ey), linear)
    pxy = pxy.reshape(rows, pairs * 4).astype(np.float32)
    pz = np.einsum("kc,eE->cEek", linear, eye_z).reshape(2 * ez, sz)
    pz = np.tile(pz, (pairs * 4, 1)).astype(np.float32)

    operands = {
        "res": residual_local.reshape(rows, sz),
        "geo": geometry.reshape(3, rows, sz),
        "hel": helmholtz.reshape(rows, sz),
        "ids": coarse_ids.transpose(0, 1, 3, 2).reshape(pairs, 8, ez),
        "dy": left_table(np.kron(eye_y, derivative)),
        "dyt": left_table(np.kron(eye_y, derivative.T)),
        "sqy": left_table(np.kron(eye_y, square.T)),
        "dz": right_table(np.kron(eye_z, derivative.T)),
        "dzt": right_table(np.kron(eye_z, derivative)),
        "sqz": right_table(np.kron(eye_z, square)),
        "pxy": pxy,
        "pxyt": np.ascontiguousarray(pxy.T),
        "pz": pz,
    }
    operands = [jnp.asarray(operands[name]) for name in ORDER]
    coarse_row = coarse_correction.reshape(1, slots)
    if padded != slots:
        coarse_row = jnp.pad(coarse_row, ((0, 0), (0, padded - slots)))

    f32 = jnp.float32
    dma = pltpu.SemaphoreType.DMA
    vmem = pl.BlockSpec(memory_space=pltpu.VMEM)
    out, coarse = pl.pallas_call(
        functools.partial(kernel, (nw, nn, sx, sy, sz, slots, padded), derivative),
        out_shape=(
            pltpu.VMEM((rows, sz), f32),
            pltpu.VMEM((1, padded), f32),
        ),
        in_specs=[vmem] + [pl.BlockSpec(memory_space=pl.ANY)] * len(ORDER),
        out_specs=(vmem, vmem),
        scratch_shapes=[
            *(pltpu.VMEM(o.shape, o.dtype) for o in operands),
            dma((len(ORDER),)),
            pltpu.VMEM((FIELDS, rows, sz), f32),
            pltpu.VMEM((FIELDS, 2, sy, sz), f32),
            pltpu.VMEM((FIELDS, 2, sx, sz), f32),
            pltpu.VMEM((FIELDS, 2, sy, sz), f32),
            pltpu.VMEM((FIELDS, 2, sx, sz), f32),
            pltpu.VMEM((FIELDS, 4, 1, sz), f32),
            pltpu.VMEM((3, rows, sz), f32),
            pltpu.VMEM((2, 3, sy, sz), f32),
            pltpu.VMEM((2, 3, sy, sz), f32),
            pltpu.VMEM((pairs * 8 * ez, nn * padded), jnp.bfloat16),
            pltpu.VMEM((1, padded), f32),
            pltpu.VMEM((nn, 1, padded), f32),
            pltpu.VMEM((nn, 1, padded), f32),
            pltpu.VMEM((nn, 1, padded), f32),
            dma((FIELDS, len(DIRS))),
            dma((FIELDS, len(DIRS))),
            dma((nn,)),
            dma((nn,)),
            dma((nn,)),
            dma((nn,)),
            dma((2,)),
            dma((2,)),
        ],
        compiler_params=pltpu.CompilerParams(collective_id=0, has_side_effects=True),
    )(
        coarse_row,
        *operands,
    )
    return out.reshape(sx, sy, sz), coarse[:, :slots].reshape(slots)


def solution(mesh):
    return jax.shard_map(
        functools.partial(on_device, mesh.shape["wide"], mesh.shape["narrow"]),
        mesh=mesh,
        in_specs=(
            P("wide", "narrow", None),
            P(None, "wide", "narrow", None),
            P("wide", "narrow", None),
            P("wide", "narrow", None, None),
            P(("wide", "narrow")),
        ),
        out_specs=(P("wide", "narrow", None), P(("wide", "narrow"))),
        check_vma=False,
    )
```

```python
import functools
import math

import jax
import jax.numpy as jnp
import numpy as np
from jax import lax
from jax.experimental import pallas as pl
from jax.experimental.pallas import tpu as pltpu
from jax.sharding import PartitionSpec as P

NODES = 8
DEGREE = 3
MESH = pl.DeviceIdType.MESH
HIGHEST = lax.Precision.HIGHEST

low_bound = 0.3
high_bound = 3.3
gll_inner = (
    -0.8717401485096066,
    -0.5917001814331423,
    -0.2092992179024789,
    0.2092992179024789,
    0.5917001814331423,
    0.8717401485096066,
)

DIRS = ((-1, 0), (1, 0), (-1, -1), (-1, 1), (1, -1), (1, 1), (0, -1), (0, 1))
X_DIRS, Y_DIRS, X_ONLY = (0, 1, 2, 3, 4, 5), (6, 7), (0, 1)
OPPOSITE = tuple(DIRS.index((-a, -b)) for a, b in DIRS)

DIAG, RES, CORR, GEO_X, GEO_Y, GEO_Z, MASS, FIRST = range(8)
FIELDS = FIRST + 2 * DEGREE - 1


def legendre_values(points, order):
    previous = points * 0.0 + 1.0
    current = points
    for number in range(1, order):
        previous, current = (
            current,
            ((2 * number + 1) * points * current - number * previous) / (number + 1),
        )
    return current


def tables():
    order = NODES - 1
    points = np.concatenate([np.array([-1.0]), np.array(gll_inner), np.array([1.0])])
    values = legendre_values(points, order)
    eye = np.eye(NODES)
    differ = points[:, None] - points[None, :] + eye
    offdiag = np.where(eye > 0, 0.0, values[:, None] / values[None, :] / differ)
    ends = np.concatenate(
        [
            np.array([-order * (order + 1) / 4.0]),
            np.zeros(NODES - 2),
            np.array([order * (order + 1) / 4.0]),
        ]
    )
    derivative = offdiag + eye * ends[None, :]
    linear = np.stack([(1.0 - points) / 2.0, (1.0 + points) / 2.0], axis=1)
    return derivative.astype(np.float32), linear.astype(np.float32)


def chain(length):
    matrix = np.eye(length)
    for place in range(NODES, length, NODES):
        matrix[place - 1, place] = matrix[place, place - 1] = 1.0
    return matrix


def halves(matrix):
    matrix = matrix.astype(np.float32)
    high = matrix.astype(jnp.bfloat16)
    low = (matrix - high.astype(np.float32)).astype(jnp.bfloat16)
    return high, low


def left_table(matrix):
    return np.stack(halves(matrix))


def right_table(matrix):
    high, low = halves(matrix)
    return np.block([[high, low], [high, np.zeros_like(low)]])


def split(value):
    high = value.astype(jnp.bfloat16)
    low = (value - high.astype(jnp.float32)).astype(jnp.bfloat16)
    return high, low


def dot(a, b):
    return jnp.dot(a, b, preferred_element_type=jnp.float32)


def left(table, value):
    high, low = split(value)
    n = value.shape[1]
    both = dot(table[0], jnp.concatenate([high, low], axis=1))
    return both[:, :n] + both[:, n:] + dot(table[1], high)


def right(value, table):
    high, low = split(value)
    n = value.shape[1]
    both = dot(jnp.concatenate([high, low], axis=1), table[...])
    return both[:, :n] + both[:, n:]


def directions(field):
    if field == GEO_X:
        return Y_DIRS
    if field == GEO_Y:
        return X_ONLY
    return (*X_ONLY, *Y_DIRS) if field >= FIRST else (*X_DIRS, *Y_DIRS)


ORDER = ("hel", "res", "geo", "sqz", "sqy", "ids", "pz", "pxy", "dz", "dy", "dzt", "dyt", "pxyt", "sdzt", "sdyt")


def three_rows(row):
    high = row.astype(jnp.bfloat16).astype(jnp.float32)
    rest = row - high
    mid = rest.astype(jnp.bfloat16).astype(jnp.float32)
    low = rest - mid
    place = lax.broadcasted_iota(jnp.int32, (8, row.shape[1]), 0)
    zero = jnp.zeros((8, row.shape[1]), jnp.float32)
    return jnp.where(
        place == 0, high, jnp.where(place == 1, mid, jnp.where(place == 2, low, zero))
    ).astype(jnp.bfloat16)


def kernel(
    sizes,
    derivative,
    cc_ref,
    *refs,
):
    count = len(ORDER)
    outside, (out_ref, coarse_ref), inside = refs[:count], refs[count : count + 2], refs[count + 2 :]
    body(sizes, derivative, outside, cc_ref, out_ref, coarse_ref, inside[:count], *inside[count:])


def body(
    sizes,
    derivative,
    outside,
    cc_ref,
    out_ref,
    coarse_ref,
    inside,
    load_sem,
    fbuf,
    xs,
    ys,
    xr,
    yr,
    dr,
    tsend,
    trecv,
    onehot,
    csend,
    crecv,
    psend,
    precv,
    send_sem,
    recv_sem,
    csend_sem,
    crecv_sem,
    psend_sem,
    precv_sem,
    tsend_sem,
    trecv_sem,
):
    nw, nn, sx, sy, sz, slots, padded = sizes
    rows = sx * sy
    w, n = lax.axis_index("wide"), lax.axis_index("narrow")
    ez = sz // NODES
    pairs = (sx // NODES) * (sy // NODES)

    def exists(step):
        dw, dn = step
        cond = None
        for place, move, count in ((w, dw, nw), (n, dn, nn)):
            if move:
                here = place > 0 if move < 0 else place < count - 1
                cond = here if cond is None else jnp.logical_and(cond, here)
        return cond

    loads = {
        name: pltpu.make_async_copy(outside[i], inside[i], load_sem.at[i])
        for i, name in enumerate(ORDER)
    }
    at = dict(zip(ORDER, inside))
    res_ref, geo_ref, hel_ref, ids_ref = at["res"], at["geo"], at["hel"], at["ids"]
    dy_ref, dyt_ref, sqy_ref = at["dy"], at["dyt"], at["sqy"]
    dz_ref, dzt_ref, sqz_ref = at["dz"], at["dzt"], at["sqz"]
    sdyt_ref, sdzt_ref = at["sdyt"], at["sdzt"]
    pxy_ref, pxyt_ref, pz_ref = at["pxy"], at["pxyt"], at["pz"]

    def loaded(*names):
        for name in names:
            loads[name].wait()

    barrier = pltpu.get_barrier_semaphore()
    for step in DIRS[:6]:

        @pl.when(exists(step))
        def _():
            pl.semaphore_signal(
                barrier, inc=1, device_id=(w + step[0], n + step[1]), device_id_type=MESH
            )

    for j in range(1, nn):
        pl.semaphore_signal(
            barrier, inc=1, device_id=(w, lax.rem(n + j, nn)), device_id_type=MESH
        )

    for name in ORDER:
        loads[name].start()

    def barrier_wait():
        peers = nn - 1
        for step in DIRS[:6]:
            peers = peers + jnp.where(exists(step), 1, 0)
        pl.semaphore_wait(barrier, peers)

    def buffers(field, k):
        dw, dn = DIRS[k]
        xside, yside = int(dw > 0), int(dn > 0)
        o = OPPOSITE[k]
        if dn == 0:
            return xs.at[field, xside], xr.at[field, int(DIRS[o][0] > 0)]
        if dw == 0:
            return ys.at[field, yside], yr.at[field, int(DIRS[o][1] > 0)]
        line = sy - 1 if dn > 0 else 0
        return xs.at[field, xside, pl.ds(line, 1)], dr.at[field, o - 2]

    def descriptor(field, k):
        source, target = buffers(field, k)
        return pltpu.make_async_remote_copy(
            src_ref=source,
            dst_ref=target,
            send_sem=send_sem.at[field, k],
            recv_sem=recv_sem.at[field, OPPOSITE[k]],
            device_id=(w + DIRS[k][0], n + DIRS[k][1]),
            device_id_type=MESH,
        )

    lane = lax.broadcasted_iota(jnp.int32, (1, sz), 1)
    z_low = jnp.logical_and(lane % NODES == 0, lane > 0)
    z_high = jnp.logical_and(lane % NODES == NODES - 1, lane < sz - 1)
    sub = lax.broadcasted_iota(jnp.int32, (1, NODES, 1), 1)

    def sum_z(value):
        return (
            value
            + jnp.where(z_low, pltpu.roll(value, 1, 1), 0.0)
            + jnp.where(z_high, pltpu.roll(value, sz - 1, 1), 0.0)
        )

    def sum_y(value):
        cube = value.reshape(sx, sy // NODES, NODES, sz)
        parts = []
        count = sy // NODES
        for e in range(count):
            block = cube[:, e]
            if e > 0:
                block = block + jnp.where(sub == 0, pltpu.roll(cube[:, e - 1], 1, 1), 0.0)
            if e < count - 1:
                block = block + jnp.where(
                    sub == NODES - 1, pltpu.roll(cube[:, e + 1], NODES - 1, 1), 0.0
                )
            parts.append(block)
        return jnp.stack(parts, axis=1).reshape(rows, sz)

    def sum_x(value):
        cube = value.reshape(sx, sy, sz)
        planes = []
        for x in range(sx):
            plane = cube[x]
            if x % NODES == 0 and x > 0:
                plane = plane + cube[x - 1]
            if x % NODES == NODES - 1 and x < sx - 1:
                plane = plane + cube[x + 1]
            planes.append(plane)
        return jnp.stack(planes, axis=0).reshape(rows, sz)

    def store_x(field, value):
        xs[field, 0] = value[:sy]
        xs[field, 1] = value[rows - sy :]

    def prepare(field, value):
        fbuf[field] = value
        if 0 in directions(field) and field < FIRST:
            store_x(field, value)
        if 6 in directions(field):
            ys[field, 0] = fbuf[field, pl.ds(0, sx, stride=sy), :]
            ys[field, 1] = fbuf[field, pl.ds(sy - 1, sx, stride=sy), :]

    def send(field, ks):
        for k in ks:

            @pl.when(exists(DIRS[k]))
            def _():
                descriptor(field, k).start()

    def finish(field, ks):
        for k in ks:
            dw, dn = DIRS[k]

            @pl.when(exists(DIRS[k]))
            def _():
                descriptor(field, OPPOSITE[k]).wait_recv()
                first = 0 if dw < 0 else rows - sy
                if dn == 0:
                    fbuf[field, pl.ds(first, sy), :] += xr[field, int(dw > 0)]
                elif dw == 0:
                    line = 0 if dn < 0 else sy - 1
                    fbuf[field, pl.ds(line, sx, stride=sy), :] += yr[field, int(dn > 0)]
                else:
                    line = first + (0 if dn < 0 else sy - 1)
                    fbuf[field, pl.ds(line, 1), :] += dr[field, k - 2]

    def patch(value, faces):
        return jnp.concatenate([faces[:sy], value[sy : rows - sy], faces[sy:]], axis=0)

    def faces_of(value):
        return jnp.concatenate([value[:sy], value[rows - sy :]], axis=0)

    def face_part(field):
        return jnp.concatenate(
            [fbuf[field, pl.ds(0, sy), :], fbuf[field, pl.ds(rows - sy, sy), :]], axis=0
        )

    def inner_terms(field, value):
        planes = []
        for base, face in ((0, 0), (sx - NODES, NODES - 1)):
            total = None
            for a in range(NODES):
                inner = None
                for b in range(NODES):
                    entry = float(derivative[a, b])
                    if b == face or entry == 0.0:
                        continue
                    term = entry * value[(base + b) * sy : (base + b + 1) * sy]
                    inner = term if inner is None else inner + term
                entry = float(derivative[a, face])
                if inner is None or entry == 0.0:
                    continue
                term = entry * fbuf[GEO_X, pl.ds((base + a) * sy, sy), :] * inner
                total = term if total is None else total + term
            planes.append(total)
        xs[field, 0], xs[field, 1] = planes
        send(field, X_ONLY)

    def table_copy(k):
        o = OPPOSITE[k]
        return pltpu.make_async_remote_copy(
            src_ref=tsend.at[k],
            dst_ref=trecv.at[o],
            send_sem=tsend_sem.at[k],
            recv_sem=trecv_sem.at[o],
            device_id=(w + DIRS[k][0], n),
            device_id_type=MESH,
        )

    def along_x(value, matrix):
        cube = value.reshape(sx // NODES, NODES, sy, sz)
        out = []
        for a in range(NODES):
            total = None
            for b in range(NODES):
                entry = float(matrix[a, b])
                if entry == 0.0:
                    continue
                term = entry * cube[:, b]
                total = term if total is None else total + term
            out.append(total)
        return jnp.stack(out, axis=1).reshape(rows, sz)

    def element_operator(value, second, third, mass):
        gx = along_x(value, derivative) * geo_ref[0]
        gy = left(dy_ref, value) * second[...]
        gz = right(value, dz_ref) * third[...]
        return (
            along_x(gx, derivative.T)
            + left(dyt_ref, gy)
            + right(gz, dzt_ref)
            + mass[...] * value
        )

    loaded("hel", "res")
    prepare(RES, sum_x(sum_y(sum_z(res_ref[...]))))
    loaded("geo", "sqz", "sqy")
    square = derivative * derivative
    diagonal = (
        along_x(geo_ref[0], square.T)
        + left(sqy_ref, geo_ref[1])
        + right(geo_ref[2], sqz_ref)
        + hel_ref[...]
    )
    prepare(DIAG, sum_x(sum_y(sum_z(diagonal))))
    prepare(GEO_X, sum_y(sum_z(geo_ref[0])))
    csend[...] = cc_ref[...]
    lanes = lax.broadcasted_iota(jnp.int32, (1, padded), 1)
    values = []
    for j in range(nn):
        owner = lax.rem(n - j + nn, nn)
        values.append(jnp.where(lanes < slots, owner * slots + lanes, -1))
    numbers = jnp.concatenate(values, axis=1)
    loaded("ids")
    for pair in range(pairs):
        block = ids_ref[pair].T
        for v in range(8):
            onehot[pl.ds((pair * 8 + v) * ez, ez), :] = jnp.where(
                block[:, v : v + 1] == numbers, 1.0, 0.0
            ).astype(jnp.bfloat16)

    barrier_wait()

    def coarse_copy(source, target, sems, rsems, j):
        peer = lax.rem(n + j, nn)
        return pltpu.make_async_remote_copy(
            src_ref=source,
            dst_ref=target,
            send_sem=sems.at[j],
            recv_sem=rsems.at[j],
            device_id=(w, peer),
            device_id_type=MESH,
        )

    for j in range(1, nn):
        coarse_copy(csend, crecv.at[j], csend_sem, crecv_sem, j).start()
    for field in (DIAG, RES, GEO_X):
        send(field, Y_DIRS)
    for field in (DIAG, RES):
        send(field, X_DIRS)
    prepare(GEO_Y, sum_x(sum_z(geo_ref[1])))
    prepare(GEO_Z, sum_x(sum_y(geo_ref[2])))
    prepare(MASS, sum_x(sum_y(sum_z(hel_ref[...]))))
    send(GEO_Y, X_ONLY)
    for field in (GEO_Z, MASS):
        send(field, (*X_DIRS, *Y_DIRS))

    theta = 0.5 * (high_bound + low_bound)
    delta = 0.5 * (high_bound - low_bound)
    sigma = theta / delta

    finish(DIAG, Y_DIRS)
    finish(RES, Y_DIRS)
    finish(GEO_X, Y_DIRS)
    inverse = 1.0 / fbuf[DIAG]
    residual = fbuf[RES]
    update = inverse * residual * (1.0 / theta)
    inner_terms(FIRST, update)
    for side, base, face in ((0, 0, 0), (1, sx - NODES, NODES - 1)):
        total = None
        for a in range(NODES):
            entry = float(derivative[a, face]) ** 2
            term = entry * fbuf[GEO_X, pl.ds((base + a) * sy, sy), :]
            total = term if total is None else total + term
        tsend[side, 0] = total
    for k in (0, 1):

        @pl.when(exists(DIRS[k]))
        def _():
            table_copy(k).start()


    loaded(*ORDER[ORDER.index("ids") + 1 :])

    finish(GEO_Y, X_ONLY)
    for field in (GEO_Z, MASS):
        finish(field, (*Y_DIRS, *X_DIRS))
    for k, first in ((0, 0), (1, rows - sy)):

        @pl.when(exists(DIRS[k]))
        def _():
            table_copy(OPPOSITE[k]).wait_recv()
            fbuf[MASS, pl.ds(first, sy), :] += trecv[k, 0]

    finish(DIAG, X_DIRS)
    finish(RES, X_DIRS)
    inverse_faces = 1.0 / face_part(DIAG)
    residual_faces = face_part(RES)
    inverse = patch(inverse, inverse_faces)
    residual = patch(residual, residual_faces)
    update = patch(update, inverse_faces * residual_faces * (1.0 / theta))

    rho = 1.0 / sigma
    solution_value = jnp.zeros((rows, sz), jnp.float32)
    count = 2 * DEGREE - 1
    for number in range(count):
        solution_value = solution_value + update
        field = FIRST + number
        prepare(field, left(sdyt_ref, left(dy_ref, update) * fbuf[GEO_Y]))
        send(field, Y_DIRS)
        fbuf[field] += (
            sum_x(along_x(along_x(update, derivative) * fbuf[GEO_X], derivative.T))
            + right(right(update, dz_ref) * fbuf[GEO_Z], sdzt_ref)
            + fbuf[MASS] * update
        )
        if number == DEGREE - 1:
            finish(CORR, (*Y_DIRS, *X_DIRS))
        finish(field, Y_DIRS)

        old_residual, old_update = residual, update
        residual = old_residual - fbuf[field]
        if number == DEGREE - 1:
            image = fbuf[CORR]
            shifted = residual - image
            update = inverse * shifted * (1.0 / theta)
        else:
            rho_next = 1.0 / (2.0 * sigma - rho)
            keep, gain = rho_next * rho, 2.0 * rho_next / delta
            rho = rho_next
            update = keep * old_update + gain * inverse * residual
        if number + 1 < count:
            inner_terms(field + 1, update)
        if number == 0:
            pieces = [csend[...]]
            for j in range(1, nn):
                coarse_copy(csend, crecv.at[j], csend_sem, crecv_sem, j).wait_recv()
                pieces.append(crecv[j])
            whole = jnp.concatenate(pieces, axis=1)
            contract_last = (((1,), (1,)), ((), ()))
            picked = jnp.sum(
                lax.dot_general(
                    three_rows(whole), onehot[...], contract_last, preferred_element_type=jnp.float32
                ),
                axis=0,
                keepdims=True,
            )
            columns = pairs * 8 * ez
            groups = pairs * 4
            row_of = lax.broadcasted_iota(jnp.int32, (groups, columns), 1) // (2 * ez)
            mine = row_of == lax.broadcasted_iota(jnp.int32, (groups, columns), 0)
            spread = jnp.where(mine, picked, 0.0)
            along_z = jnp.dot(
                spread, pz_ref[...], precision=HIGHEST, preferred_element_type=jnp.float32
            )
            correction = jnp.dot(
                pxy_ref[...], along_z, precision=HIGHEST, preferred_element_type=jnp.float32
            )
            product = element_operator(correction, geo_ref.at[1], geo_ref.at[2], hel_ref)
            prepare(CORR, sum_x(sum_y(sum_z(product))))
            send(CORR, (*Y_DIRS, *X_DIRS))
        if number == DEGREE:
            point = lax.broadcasted_iota(jnp.int32, (rows, sz), 0)
            x, y = point // sy, point % sy
            z = lax.broadcasted_iota(jnp.int32, (rows, sz), 1)
            weighted = pre_residual
            for local, start, total in (
                (x, w * sx, nw * sx),
                (y, n * sy, nn * sy),
                (z, 0, sz),
            ):
                spot = start + local
                inner = jnp.logical_or(
                    jnp.logical_and(local % NODES == 0, spot > 0),
                    jnp.logical_and(local % NODES == NODES - 1, spot < total - 1),
                )
                weighted = weighted * jnp.where(inner, 0.5, 1.0)
            on_xy = jnp.dot(
                pxyt_ref[...], weighted, precision=HIGHEST, preferred_element_type=jnp.float32
            )
            on_z = lax.dot_general(
                on_xy,
                pz_ref[...],
                contract_last,
                precision=HIGHEST,
                preferred_element_type=jnp.float32,
            )
            corners = jnp.sum(jnp.where(mine, on_z, 0.0), axis=0, keepdims=True)
            partial = jnp.sum(dot(three_rows(corners), onehot[...]), axis=0, keepdims=True)
            for j in range(1, nn):
                at = (nn - j) * padded
                psend[j] = partial[:, at : at + padded]
                coarse_copy(psend.at[j], precv.at[j], psend_sem, precv_sem, j).start()
            own = partial[:, :padded]
        finish(field, X_ONLY)
        residual_faces = faces_of(old_residual) - face_part(field)
        residual = patch(residual, residual_faces)
        if number == DEGREE - 1:
            pre_residual = residual
            shifted_faces = residual_faces - faces_of(image)
            residual = patch(shifted, shifted_faces)
            update = patch(update, inverse_faces * shifted_faces * (1.0 / theta))
            rho = 1.0 / sigma
        else:
            update = patch(
                update, keep * faces_of(old_update) + gain * inverse_faces * residual_faces
            )
    solution_value = correction + solution_value + update
    out_ref[...] = solution_value

    for j in range(1, nn):
        coarse_copy(psend.at[j], precv.at[j], psend_sem, precv_sem, j).wait_recv()
        own = own + precv[j]
    coarse_ref[...] = own

    for j in range(1, nn):
        coarse_copy(csend, crecv.at[j], csend_sem, crecv_sem, j).wait_send()
        coarse_copy(psend.at[j], precv.at[j], psend_sem, precv_sem, j).wait_send()
    for field in range(FIELDS):
        for k in directions(field):

            @pl.when(exists(DIRS[k]))
            def _():
                descriptor(field, k).wait_send()

    for k in (0, 1):

        @pl.when(exists(DIRS[k]))
        def _():
            table_copy(k).wait_send()


def on_device(nw, nn, residual_local, geometry, helmholtz, coarse_ids, coarse_correction):
    derivative, linear = tables()
    sx, sy, sz = residual_local.shape
    rows = sx * sy
    slots = coarse_correction.shape[0]
    padded = -(-slots // 128) * 128
    ex, ey, ez = sx // NODES, sy // NODES, sz // NODES
    pairs = ex * ey
    square = derivative * derivative
    eye_y, eye_z = np.eye(rows // NODES), np.eye(ez)

    pxy = np.einsum("eE,ia,fF,jb->eifjEFab", np.eye(ex), linear, np.eye(ey), linear)
    pxy = pxy.reshape(rows, pairs * 4).astype(np.float32)
    pz = np.einsum("kc,eE->cEek", linear, eye_z).reshape(2 * ez, sz)
    pz = np.tile(pz, (pairs * 4, 1)).astype(np.float32)

    operands = {
        "res": residual_local.reshape(rows, sz),
        "geo": geometry.reshape(3, rows, sz),
        "hel": helmholtz.reshape(rows, sz),
        "ids": coarse_ids.transpose(0, 1, 3, 2).reshape(pairs, 8, ez),
        "dy": left_table(np.kron(eye_y, derivative)),
        "dyt": left_table(np.kron(eye_y, derivative.T)),
        "sqy": left_table(np.kron(eye_y, square.T)),
        "dz": right_table(np.kron(eye_z, derivative.T)),
        "dzt": right_table(np.kron(eye_z, derivative)),
        "sqz": right_table(np.kron(eye_z, square)),
        "sdyt": left_table(np.kron(np.eye(sx), chain(sy)) @ np.kron(eye_y, derivative.T)),
        "sdzt": right_table(np.kron(eye_z, derivative) @ chain(sz)),
        "pxy": pxy,
        "pxyt": np.ascontiguousarray(pxy.T),
        "pz": pz,
    }
    operands = [jnp.asarray(operands[name]) for name in ORDER]
    coarse_row = coarse_correction.reshape(1, slots)
    if padded != slots:
        coarse_row = jnp.pad(coarse_row, ((0, 0), (0, padded - slots)))

    f32 = jnp.float32
    dma = pltpu.SemaphoreType.DMA
    vmem = pl.BlockSpec(memory_space=pltpu.VMEM)
    out, coarse = pl.pallas_call(
        functools.partial(kernel, (nw, nn, sx, sy, sz, slots, padded), derivative),
        out_shape=(
            pltpu.VMEM((rows, sz), f32),
            pltpu.VMEM((1, padded), f32),
        ),
        in_specs=[vmem] + [pl.BlockSpec(memory_space=pl.ANY)] * len(ORDER),
        out_specs=(vmem, vmem),
        scratch_shapes=[
            *(pltpu.VMEM(o.shape, o.dtype) for o in operands),
            dma((len(ORDER),)),
            pltpu.VMEM((FIELDS, rows, sz), f32),
            pltpu.VMEM((FIELDS, 2, sy, sz), f32),
            pltpu.VMEM((FIELDS, 2, sx, sz), f32),
            pltpu.VMEM((FIELDS, 2, sy, sz), f32),
            pltpu.VMEM((FIELDS, 2, sx, sz), f32),
            pltpu.VMEM((FIELDS, 4, 1, sz), f32),
            pltpu.VMEM((2, 1, sy, sz), f32),
            pltpu.VMEM((2, 1, sy, sz), f32),
            pltpu.VMEM((pairs * 8 * ez, nn * padded), jnp.bfloat16),
            pltpu.VMEM((1, padded), f32),
            pltpu.VMEM((nn, 1, padded), f32),
            pltpu.VMEM((nn, 1, padded), f32),
            pltpu.VMEM((nn, 1, padded), f32),
            dma((FIELDS, len(DIRS))),
            dma((FIELDS, len(DIRS))),
            dma((nn,)),
            dma((nn,)),
            dma((nn,)),
            dma((nn,)),
            dma((2,)),
            dma((2,)),
        ],
        compiler_params=pltpu.CompilerParams(collective_id=0, has_side_effects=True),
    )(
        coarse_row,
        *operands,
    )
    return out.reshape(sx, sy, sz), coarse[:, :slots].reshape(slots)


def solution(mesh):
    return jax.shard_map(
        functools.partial(on_device, mesh.shape["wide"], mesh.shape["narrow"]),
        mesh=mesh,
        in_specs=(
            P("wide", "narrow", None),
            P(None, "wide", "narrow", None),
            P("wide", "narrow", None),
            P("wide", "narrow", None, None),
            P(("wide", "narrow")),
        ),
        out_specs=(P("wide", "narrow", None), P(("wide", "narrow"))),
        check_vma=False,
    )
```
